256 devices in a mesh: front: 4 (over y_lo, core), blk: 64 (over y_hi, x, z).
Axes of the slice: x: 4, y: 4 (y_hi: 2, y_lo: 2; y = y_hi * 2 + y_lo), z: 8, core: 2. Of those that a mesh axis runs over, the one named last changes fastest.
Arguments:
- front: float32 [4, 8192, 8192], P('front', 'blk'), parts along dimension 0, may hold values from -8 to 40, as said below
- child: float32 [4, 4096, 4096], P('front', 'blk'), parts along dimension 0, may hold values from -1 to 4, as said below
- index_map: int32 [16384], P('front'), parts along dimension 0, may hold values from 0 to 8191, as said below
Outputs:
- factored: float32 [4, 8192, 8192], P('front', 'blk'), parts along dimension 0
The draws below stay inside these ranges and needn't reach their ends.
There are 4 independent parts, one for each index of `front`. The reference program is written for one: setup_inputs(seed, part) draws one part's arguments, and reference() takes and returns one part's arrays. A program takes and returns all parts, laid end to end along the dimension named above; each array names one. Nothing has to cross between parts.
Inputs may be any that keep to these rules, and one draw needn't show every extreme that they name: front is symmetric and positive definite. child is symmetric and positive semidefinite. `index_map`: tile t of the child (indices t * 64 to t * 64 + 63, with t = k * 64 + e and e < 64) maps in increasing order onto 64 different indices of the front's block column b = k * 64 + ((e + h) mod 64), where h is half of 64, that is onto indices b * 128 to b * 128 + 127; no two child indices share a front index.
All inputs are finite; a program needn't handle non-finite values.
Results may differ from the reference program's by a relative error of at most 0.0034.
Values may be sent and summed in bfloat16 or wider, within the bound.
A program may use at most 128 MiB of HBM per device.

```python
import math
import jax
import jax.numpy as jnp
from jax import lax

PANEL_WIDTH = 512
BLOCK_WIDTH = 128
COL_BLOCKS = 1
FRONT_ORDER = 8192
CHILD_ORDER = 4096
TILE_WIDTH = 64
N_BLK = 64


def symmetric_noise(subkey, matrix_order, spread):
    normal_draw = jax.random.normal(subkey, (matrix_order, matrix_order), jnp.float32)
    return (normal_draw + normal_draw.T) * (spread / math.sqrt(2.0))


def draw_front(key, part):
    subkeys = jax.random.split(jax.random.fold_in(key, 101), 2)
    coupling_rank = 2 * PANEL_WIDTH
    coupling = jax.random.normal(subkeys[0], (FRONT_ORDER, coupling_rank), jnp.float32)
    coupling = coupling * (2.0 / math.sqrt(coupling_rank))
    matrix = jnp.dot(coupling, coupling.T, precision=lax.Precision.HIGHEST)
    matrix = matrix + symmetric_noise(subkeys[1], FRONT_ORDER, 0.25 / math.sqrt(FRONT_ORDER))
    matrix = matrix + jnp.eye(FRONT_ORDER, dtype=jnp.float32)
    return matrix.reshape(COL_BLOCKS, N_BLK * BLOCK_WIDTH, FRONT_ORDER)


def draw_child(key, part):
    subkeys = jax.random.split(jax.random.fold_in(key, 202), 2)
    levels = jax.random.uniform(subkeys[0], (CHILD_ORDER,), jnp.float32, 1.5, 3.0)
    matrix = jnp.diag(levels) + symmetric_noise(subkeys[1], CHILD_ORDER, 0.5 / math.sqrt(CHILD_ORDER))
    return matrix.reshape(COL_BLOCKS, N_BLK * TILE_WIDTH, CHILD_ORDER)


def pick_subset(subkey):
    return jax.random.permutation(subkey, BLOCK_WIDTH)[:TILE_WIDTH]


def draw_index_map(key, part):
    tile_count = FRONT_ORDER // BLOCK_WIDTH
    subkeys = jax.random.split(jax.random.fold_in(key, 303), tile_count)
    chosen = jnp.sort(jax.vmap(pick_subset)(subkeys).astype(jnp.int32), axis=1)
    tile_ids = jnp.arange(tile_count, dtype=jnp.int32)
    target = tile_ids // N_BLK * N_BLK + (tile_ids % N_BLK + N_BLK // 2) % N_BLK
    return (target[:, None] * BLOCK_WIDTH + chosen).reshape(-1).astype(jnp.int32)


def setup_inputs(seed: int = 0, part: int = 0) -> dict:
    streams_of = jax.random.split(jax.random.key(seed), 4)
    own_keys = jax.random.split(jax.random.fold_in(streams_of[3], part), 4)
    front = draw_front(jax.random.fold_in(jax.random.fold_in(streams_of[3], part), 71), part)
    child = draw_child(jax.random.fold_in(jax.random.fold_in(streams_of[3], part), 71), part)
    index_map = draw_index_map(jax.random.fold_in(jax.random.fold_in(streams_of[3], part), 71), part)
    return dict(front=front, child=child, index_map=index_map)


def factor_rows(matrix, row_start):
    diag_factor = jnp.linalg.cholesky(matrix[row_start:row_start + PANEL_WIDTH, row_start:row_start + PANEL_WIDTH])
    panel_part = matrix[:, row_start:row_start + PANEL_WIDTH]
    solved = lax.linalg.triangular_solve(diag_factor, panel_part, left_side=False, lower=True, transpose_a=True)
    offsets = jnp.arange(FRONT_ORDER, dtype=jnp.int32) - row_start
    diag_rows = jnp.take(diag_factor, jnp.clip(offsets, 0, PANEL_WIDTH - 1), axis=0)
    inside = (offsets >= 0) & (offsets < PANEL_WIDTH)
    before = offsets < 0
    return jnp.where(inside[:, None], diag_rows, jnp.where(before[:, None], jnp.zeros((), solved.dtype), solved))

def reference(front, child, index_map):
    matrix = front.reshape(FRONT_ORDER, FRONT_ORDER)
    contribution = child.reshape(CHILD_ORDER, CHILD_ORDER)
    matrix = matrix.at[index_map[:, None], index_map[None, :]].add(contribution)
    for row_start in (0, PANEL_WIDTH):
        lowered = factor_rows(matrix, row_start).astype(jnp.bfloat16)
        cutoff = row_start + PANEL_WIDTH
        remaining = matrix[cutoff:] - jnp.dot(lowered[cutoff:].astype(jnp.float32), lowered.T.astype(jnp.float32), preferred_element_type=jnp.float32)
        matrix = jnp.concatenate([matrix[:row_start], lowered.T.astype(matrix.dtype), remaining], axis=0)
    positions = jnp.arange(FRONT_ORDER, dtype=jnp.int32)
    cleared = (positions[:, None] >= 2 * PANEL_WIDTH) & (positions[None, :] < 2 * PANEL_WIDTH)
    matrix = jnp.where(cleared, jnp.zeros((), matrix.dtype), matrix)
    return matrix.reshape(COL_BLOCKS, N_BLK * BLOCK_WIDTH, FRONT_ORDER)
```

```python
import jax
import jax.numpy as jnp
from jax import lax
from jax.experimental import pallas as pl
from jax.experimental.pallas import tpu as pltpu
from jax.sharding import PartitionSpec as P

PANEL_WIDTH = 512
BLOCK = 128
TILE_WIDTH = 64
LEAD = 2 * PANEL_WIDTH
LEAD_BLOCKS = LEAD // BLOCK
ROWS = 8
Z = 8
X = 4
PIECE = 256

HIGHEST = lax.Precision.HIGHEST
ANY = pl.BlockSpec(memory_space=pl.ANY)
VMEM = pl.BlockSpec(memory_space=pltpu.VMEM)
MIB = 1024 * 1024


def dot(a, b, dims=((1,), (0,)), precision=HIGHEST):
    return lax.dot_general(
        a, b, (dims, ((), ())), precision=precision, preferred_element_type=jnp.float32
    )


def position():
    me = lax.axis_index("blk")
    return me // (X * Z), me // Z % X, me % Z


def device(y, x, z):
    return {"blk": (y * X + lax.rem(x + X, X)) * Z + lax.rem(z + Z, Z)}


def remote(src, dst, send, recv, target):
    return pltpu.make_async_remote_copy(
        src_ref=src,
        dst_ref=dst,
        send_sem=send,
        recv_sem=recv,
        device_id=target,
        device_id_type=pl.DeviceIdType.MESH,
    )


def greet(partners):
    barrier = pltpu.get_barrier_semaphore()
    for partner in partners:
        pl.semaphore_signal(
            barrier, inc=1, device_id=partner, device_id_type=pl.DeviceIdType.MESH
        )
    pl.semaphore_wait(barrier, len(partners))


def pieces_of(s):
    edges = [s * BLOCK] + [c for c in range(PIECE, LEAD + 1, PIECE) if c > s * BLOCK]
    return list(zip(edges[:-1], edges[1:]))


def share_kernel(own_ref, out_ref, local_sem, z_send, a_send, recv):
    y, x, z = position()
    greet(
        [
            device(1 - y, x, z),
            device(y, x - 1, z),
            device(y, x + 1, z),
            device(y, x, z - 1),
            device(y, x, z + 1),
        ]
    )
    root = (y == 0) & (x == 0)

    @pl.when(root)
    def _():
        copy = pltpu.make_async_copy(own_ref, out_ref.at[z], local_sem)
        copy.start()
        copy.wait()

    def piece(s, p, send, target):
        c0, c1 = pieces_of(s)[p]
        part = out_ref.at[s, :, c0:c1]
        return remote(part, part, send, recv.at[s, p], target)

    def tree_sends(s, p):
        onward = (x == 1) if p % 2 == 0 else (x == 3)
        step = 1 if p % 2 == 0 else -1
        return [
            (root, piece(s, p, a_send.at[p, 0], device(1, x, z))),
            (x == 0, piece(s, p, a_send.at[p, 1], device(y, x + 1, z))),
            (x == 0, piece(s, p, a_send.at[p, 2], device(y, x - 1, z))),
            (onward, piece(s, p, a_send.at[p, 3], device(y, x + step, z))),
        ]

    def up_hops(s):
        return 4 if s % 2 == 0 else 3

    def ring_sends(s, p, away):
        ups = up_hops(s)
        go_up = away < ups
        go_down = (away == 0) | (away > ups + 1)
        return [
            (go_up, piece(s, p, z_send.at[s, p, 0], device(y, x, z + 1))),
            (go_down, piece(s, p, z_send.at[s, p, 1], device(y, x, z - 1))),
        ]

    def start(sends):
        for condition, copy in sends:
            pl.when(condition)(copy.start)

    def arrived(s, p):
        piece(s, p, z_send.at[s, p, 0], device(y, x, z + 1)).wait_recv()

    for s in range(LEAD_BLOCKS):

        @pl.when(z == s)
        def _(s=s):
            for p in range(len(pieces_of(s))):
                pl.when(jnp.logical_not(root))(lambda p=p: arrived(s, p))
                start(tree_sends(s, p))
                start(ring_sends(s, p, 0))

    def hop(t, carry):
        away = jnp.where(t % 2 == 1, (t + 1) // 2, Z - t // 2)
        for s in range(LEAD_BLOCKS):

            @pl.when(lax.rem(z - away + Z, Z) == s)
            def _(s=s):
                for p in range(len(pieces_of(s))):
                    arrived(s, p)
                    start(ring_sends(s, p, away))

        return carry

    lax.fori_loop(1, Z, hop, 0)

    for s in range(LEAD_BLOCKS):
        away = lax.rem(z - s + Z, Z)
        for p in range(len(pieces_of(s))):
            for condition, copy in ring_sends(s, p, away):
                pl.when(condition)(copy.wait_send)
            for condition, copy in tree_sends(s, p):
                pl.when(condition & (away == 0))(copy.wait_send)


def share(own):
    most = LEAD // PIECE
    return pl.pallas_call(
        share_kernel,
        out_shape=jax.ShapeDtypeStruct((LEAD_BLOCKS, BLOCK, LEAD), jnp.float32),
        in_specs=[ANY],
        out_specs=VMEM,
        scratch_shapes=[
            pltpu.SemaphoreType.DMA,
            pltpu.SemaphoreType.DMA((LEAD_BLOCKS, most, 2)),
            pltpu.SemaphoreType.DMA((most, 4)),
            pltpu.SemaphoreType.DMA((LEAD_BLOCKS, most)),
        ],
        compiler_params=pltpu.CompilerParams(
            collective_id=0, has_side_effects=True, vmem_limit_bytes=16 * MIB
        ),
        name="share",
    )(own)


def spread_out(x):
    return jnp.broadcast_to(x, (ROWS, BLOCK))


def refined_rsqrt(d):
    guess = lax.rsqrt(d)
    return guess * (1.5 - 0.5 * d * guess * guess)


def eliminate(parts, low, inv):
    done = []
    for r in range(ROWS):
        value = parts[r]
        for s in range(r):
            value = value - low[r][s] * done[s]
        done.append(value * inv[r])
    return done


def small_factor(cols):
    a = [[spread_out(cols[s][r : r + 1, :]) for s in range(r + 1)] for r in range(ROWS)]
    low = [[None] * ROWS for _ in range(ROWS)]
    inv = [None] * ROWS
    for s in range(ROWS):
        inv[s] = refined_rsqrt(a[s][s])
        for r in range(s + 1, ROWS):
            low[r][s] = a[r][s] * inv[s]
        for r in range(s + 1, ROWS):
            for t in range(s + 1, r + 1):
                a[r][t] = a[r][t] - low[r][s] * low[t][s]
    return low, inv


def invert_factor(a_ref, x_ref):
    row = lax.broadcasted_iota(jnp.int32, (BLOCK, BLOCK), 0)
    col = lax.broadcasted_iota(jnp.int32, (BLOCK, BLOCK), 1)
    x_ref[...] = jnp.where(row == col, 1.0, 0.0).astype(jnp.float32)
    for j in range(0, BLOCK, ROWS):
        w = a_ref[j : j + ROWS, :]
        e = x_ref[j : j + ROWS, :]
        low, inv = small_factor([spread_out(w[:, j + s : j + s + 1]) for s in range(ROWS)])
        y = eliminate([spread_out(w[r : r + 1, :]) for r in range(ROWS)], low, inv)
        f = eliminate([spread_out(e[r : r + 1, :]) for r in range(ROWS)], low, inv)
        for r in range(ROWS):
            x_ref[j + r : j + r + 1, :] = f[r][0:1, :]
        for i in range(j + ROWS, BLOCK, ROWS):
            block = a_ref[i : i + ROWS, :]
            other = x_ref[i : i + ROWS, :]
            z = eliminate(
                [spread_out(block[:, j + s : j + s + 1]) for s in range(ROWS)], low, inv
            )
            for s in range(ROWS):
                block = block - z[s] * y[s]
                other = other - z[s] * f[s]
            a_ref[i : i + ROWS, :] = block
            x_ref[i : i + ROWS, :] = other


def factor_kernel(index_ref, lead_ref, own_ref, l_ref, work, a_ref, x_ref):
    width = LEAD + BLOCK
    for s in range(LEAD_BLOCKS):
        work[s, :, 0:LEAD] = lead_ref[s]
        work[s, :, LEAD:width] = own_ref[:, s * BLOCK : (s + 1) * BLOCK].T
    per_panel = PANEL_WIDTH // BLOCK

    def step(b, carry):
        a_ref[...] = work[b, :, pl.ds(pl.multiple_of(b * BLOCK, BLOCK), BLOCK)]
        invert_factor(a_ref, x_ref)
        work[b] = dot(x_ref[...], work[b])

        def update(t, carry):
            crossing = work[b, :, pl.ds(pl.multiple_of(t * BLOCK, BLOCK), BLOCK)]
            work[t] = work[t] - dot(crossing, work[b], ((0,), (0,)))
            return carry

        lax.fori_loop(b + 1, (b // per_panel + 1) * per_panel, update, 0)

        @pl.when(b == per_panel - 1)
        def _():
            first = work[0:per_panel, :, PANEL_WIDTH:width].astype(jnp.bfloat16)
            first = first.reshape(PANEL_WIDTH, width - PANEL_WIDTH)
            for t in range(per_panel):
                rows = work[per_panel + t, :, PANEL_WIDTH:width]
                crossing = first[:, t * BLOCK : (t + 1) * BLOCK]
                work[per_panel + t, :, PANEL_WIDTH:width] = rows - dot(
                    crossing, first, ((0,), (0,)), None
                )

        return carry

    lax.fori_loop(0, LEAD_BLOCKS, step, 0)
    for s in range(LEAD_BLOCKS):
        q = lax.broadcasted_iota(jnp.int32, (BLOCK, BLOCK), 0) + s * BLOCK
        c = lax.broadcasted_iota(jnp.int32, (BLOCK, BLOCK), 1) + index_ref[0] * BLOCK
        own = jnp.where(q <= c, work[s, :, LEAD:width], 0.0)
        l_ref[:, s * BLOCK : (s + 1) * BLOCK] = own.T.astype(jnp.bfloat16)


def factor(index, lead, own):
    return pl.pallas_call(
        factor_kernel,
        out_shape=jax.ShapeDtypeStruct((BLOCK, LEAD), jnp.bfloat16),
        in_specs=[pl.BlockSpec(memory_space=pltpu.SMEM), VMEM, VMEM],
        out_specs=VMEM,
        scratch_shapes=[
            pltpu.VMEM((LEAD_BLOCKS, BLOCK, LEAD + BLOCK), jnp.float32),
            pltpu.VMEM((BLOCK, BLOCK), jnp.float32),
            pltpu.VMEM((BLOCK, BLOCK), jnp.float32),
        ],
        compiler_params=pltpu.CompilerParams(vmem_limit_bytes=32 * MIB),
        name="factor",
    )(index, lead, own)


def exchange_kernel(
    l_ref, q_ref, line, plane, made, local_sem, l_send, l_recv, p_send, p_recv, q_send, q_recv
):
    y, x, z = position()
    a = y * X + x
    A = 2 * X
    others = [lax.rem(a + i, A) for i in range(1, A)]
    greet(
        [device(y, x, z - 1), device(y, x, z + 1)]
        + [device(other // X, other % X, z) for other in others]
    )

    def rows(index, half=None):
        if half is None:
            return pl.ds(pl.multiple_of(lax.rem(index + Z, Z) * BLOCK, BLOCK), BLOCK)
        start = lax.rem(index + Z, Z) * BLOCK + half * (BLOCK // 2)
        return pl.ds(pl.multiple_of(start, BLOCK // 2), BLOCK // 2)

    own_line = pltpu.make_async_copy(l_ref, line.at[rows(z)], local_sem.at[0])
    own_plane = pltpu.make_async_copy(l_ref, plane.at[rows(a)], local_sem.at[1])
    own_line.start()
    own_plane.start()

    def line_copy(up, hop):
        sign = 1 if up else -1
        half = None if hop < Z // 2 else (0 if up else 1)
        part = line.at[rows(z - sign * (hop - 1), half)]
        at = 0 if up else 1
        return remote(
            part, part, l_send.at[at, hop - 1], l_recv.at[at, hop - 1], device(y, x, z + sign)
        )

    def line_arrival(up, hop):
        sign = 1 if up else -1
        half = None if hop < Z // 2 else (0 if up else 1)
        part = line.at[rows(z - sign * hop, half)]
        at = 0 if up else 1
        return remote(
            part, part, l_send.at[at, hop - 1], l_recv.at[at, hop - 1], device(y, x, z + sign)
        )

    def plane_copy(slot, yy, source, half, target):
        part = plane.at[rows(yy * X + lax.rem(source + X, X), half)]
        return remote(part, part, p_send.at[slot], p_recv.at[slot], target)

    far = 1 - y
    right, left = device(y, x + 1, z), device(y, x - 1, z)
    over = device(far, x, z)
    sends = [
        plane_copy(0, y, x, None, over),
        plane_copy(1, y, x, None, right),
        plane_copy(2, y, x, None, left),
        plane_copy(3, far, x, None, right),
        plane_copy(4, far, x, None, left),
        plane_copy(5, y, x - 1, 0, right),
        plane_copy(6, y, x + 1, 1, left),
        plane_copy(7, far, x - 1, 0, right),
        plane_copy(8, far, x + 1, 1, left),
    ]
    arrivals = [
        plane_copy(0, far, x, None, over),
        plane_copy(1, y, x - 1, None, right),
        plane_copy(2, y, x + 1, None, left),
        plane_copy(3, far, x - 1, None, right),
        plane_copy(4, far, x + 1, None, left),
        plane_copy(5, y, x - 2, 0, right),
        plane_copy(6, y, x + 2, 1, left),
        plane_copy(7, far, x - 2, 0, right),
        plane_copy(8, far, x + 2, 1, left),
    ]
    own_line.wait()
    for up in (True, False):
        line_copy(up, 1).start()
    own_plane.wait()
    for slot in (0, 1, 2):
        sends[slot].start()

    def pass_on(hop):
        for up in (True, False):
            line_arrival(up, hop).wait_recv()
            line_copy(up, hop + 1).start()

    pass_on(1)
    arrivals[0].wait_recv()
    sends[3].start()
    sends[4].start()
    arrivals[1].wait_recv()
    sends[5].start()
    arrivals[2].wait_recv()
    sends[6].start()
    pass_on(2)
    arrivals[3].wait_recv()
    sends[7].start()
    arrivals[4].wait_recv()
    sends[8].start()
    pass_on(3)
    for slot in (5, 6, 7, 8):
        arrivals[slot].wait_recv()
    for up in (True, False):
        line_arrival(up, Z // 2).wait_recv()

    def product(other):
        j = lax.broadcasted_iota(jnp.int32, (BLOCK, LEAD), 0) + z * BLOCK
        q = lax.broadcasted_iota(jnp.int32, (BLOCK, LEAD), 1)
        chosen = jnp.where(j == q, 1.0, 0.0).astype(jnp.bfloat16)
        is_lead = jnp.full((BLOCK, LEAD), other, jnp.int32) == 0
        left_side = jnp.where(is_lead, chosen, plane[rows(other)])
        return dot(left_side, line[...], ((1,), (1,)), None)

    def part_of(index):
        return pl.ds(pl.multiple_of(index * LEAD, LEAD), LEAD)

    def product_copy(i):
        other = lax.rem(a + i, A)
        return remote(
            made.at[i],
            q_ref.at[:, part_of(a)],
            q_send.at[i],
            q_recv.at[i],
            device(other // X, lax.rem(other, X), z),
        )

    def make(i, carry):
        made[i] = product(lax.rem(a + i, A))

        @pl.when(i > 1)
        def _():
            product_copy(i - 1).start()

        return carry

    lax.fori_loop(1, A, make, 0)
    q_ref[:, part_of(a)] = product(a)
    product_copy(A - 1).start()
    for i in range(1, A):
        product_copy(i).wait()
    for up in (True, False):
        for hop in range(1, Z // 2 + 1):
            line_copy(up, hop).wait_send()
    for copy in sends:
        copy.wait_send()


def exchange(rows, order):
    dma = pltpu.SemaphoreType.DMA
    return pl.pallas_call(
        exchange_kernel,
        out_shape=jax.ShapeDtypeStruct((BLOCK, order), jnp.float32),
        in_specs=[ANY],
        out_specs=VMEM,
        scratch_shapes=[
            pltpu.VMEM((LEAD, LEAD), jnp.bfloat16),
            pltpu.VMEM((LEAD, LEAD), jnp.bfloat16),
            pltpu.VMEM((2 * X, BLOCK, LEAD), jnp.float32),
            dma((2,)),
            dma((2, Z // 2)),
            dma((2, Z // 2)),
            dma((9,)),
            dma((9,)),
            dma((2 * X,)),
            dma((2 * X,)),
        ],
        compiler_params=pltpu.CompilerParams(
            collective_id=1, has_side_effects=True, vmem_limit_bytes=32 * MIB
        ),
        name="exchange",
    )(rows)


def from_behind(shard, by):
    count = lax.axis_size("blk")
    return lax.ppermute(shard, "blk", [(i, (i + by) % count) for i in range(count)])


def contribution(tiles, places, own_places):
    slots = jnp.arange(BLOCK, dtype=jnp.int32)
    row_table = (places[..., None] == slots).astype(jnp.float32)
    shaped = tiles.reshape(TILE_WIDTH, -1, TILE_WIDTH)
    spread = jnp.einsum("cei,eiq->ceq", shaped, row_table, precision=HIGHEST)
    column_table = (own_places[..., None] == slots).astype(jnp.float32)
    return jnp.einsum(
        "cq,cn->qn", column_table, spread.reshape(TILE_WIDTH, -1), precision=HIGHEST
    )


def on_device(front, child, index_map):
    cycle = lax.axis_size("blk")
    half = cycle // 2
    index = lax.axis_index("blk")
    front, child = front[0], child[0]
    order = front.shape[1]
    places = (index_map % BLOCK).reshape(cycle, TILE_WIDTH)
    own_places = lax.dynamic_index_in_dim(places, (index - half) % cycle, 0, keepdims=False)
    early = slice(half * TILE_WIDTH, (half + LEAD_BLOCKS) * TILE_WIDTH)
    early_tiles = from_behind(child[:, early], half)
    own = front[:, :LEAD] + contribution(
        early_tiles, places[half : half + LEAD_BLOCKS], own_places
    )
    lead = share(own)
    lead, child = lax.optimization_barrier((lead, child))
    tiles = from_behind(child, half)
    rows = factor(index[None].astype(jnp.int32), lead, own)
    product = exchange(rows, order)
    middle = half * TILE_WIDTH
    tiles = jnp.concatenate([tiles[:, middle:], tiles[:, :middle]], axis=1)
    added = contribution(tiles, jnp.concatenate([places[half:], places[:half]]), own_places)
    remaining = jnp.where(jnp.arange(order) < LEAD, 0.0, front + added - product)
    return jnp.where(index < LEAD_BLOCKS, product, remaining)[None]


def solution(mesh):
    placed = (P("front", "blk", None), P("front", "blk", None), P("front"))
    return jax.shard_map(
        on_device, mesh=mesh, in_specs=placed, out_specs=P("front", "blk", None), check_vma=False
    )
```

```python
import jax
import jax.numpy as jnp
from jax import lax
from jax.experimental import pallas as pl
from jax.experimental.pallas import tpu as pltpu
from jax.sharding import PartitionSpec as P

PANEL_WIDTH = 512
BLOCK = 128
TILE_WIDTH = 64
LEAD = 2 * PANEL_WIDTH
LEAD_BLOCKS = LEAD // BLOCK
ROWS = 8
Z = 8
X = 4
PIECE = 256

HIGHEST = lax.Precision.HIGHEST
ANY = pl.BlockSpec(memory_space=pl.ANY)
VMEM = pl.BlockSpec(memory_space=pltpu.VMEM)
MIB = 1024 * 1024


def dot(a, b, dims=((1,), (0,)), precision=HIGHEST):
    return lax.dot_general(
        a, b, (dims, ((), ())), precision=precision, preferred_element_type=jnp.float32
    )


def position():
    me = lax.axis_index("blk")
    return me // (X * Z), me // Z % X, me % Z


def device(y, x, z):
    return {"blk": (y * X + lax.rem(x + X, X)) * Z + lax.rem(z + Z, Z)}


def remote(src, dst, send, recv, target):
    return pltpu.make_async_remote_copy(
        src_ref=src,
        dst_ref=dst,
        send_sem=send,
        recv_sem=recv,
        device_id=target,
        device_id_type=pl.DeviceIdType.MESH,
    )


def greet(partners):
    barrier = pltpu.get_barrier_semaphore()
    for partner in partners:
        pl.semaphore_signal(
            barrier, inc=1, device_id=partner, device_id_type=pl.DeviceIdType.MESH
        )
    pl.semaphore_wait(barrier, len(partners))


def pieces_of(s):
    edges = [s * BLOCK] + [c for c in range(PIECE, LEAD + 1, PIECE) if c > s * BLOCK]
    return list(zip(edges[:-1], edges[1:]))


def share_kernel(own_ref, out_ref, local_sem, z_send, a_send, recv):
    y, x, z = position()
    greet(
        [
            device(1 - y, x, z),
            device(y, x - 1, z),
            device(y, x + 1, z),
            device(y, x, z - 1),
            device(y, x, z + 1),
        ]
    )
    root = (y == 0) & (x == 0)

    @pl.when(root)
    def _():
        copy = pltpu.make_async_copy(own_ref, out_ref.at[z], local_sem)
        copy.start()
        copy.wait()

    def piece(s, p, send, target):
        c0, c1 = pieces_of(s)[p]
        part = out_ref.at[s, :, c0:c1]
        return remote(part, part, send, recv.at[s, p], target)

    def tree_sends(s, p):
        onward = (x == 1) if p % 2 == 0 else (x == 3)
        step = 1 if p % 2 == 0 else -1
        return [
            (root, piece(s, p, a_send.at[p, 0], device(1, x, z))),
            (x == 0, piece(s, p, a_send.at[p, 1], device(y, x + 1, z))),
            (x == 0, piece(s, p, a_send.at[p, 2], device(y, x - 1, z))),
            (onward, piece(s, p, a_send.at[p, 3], device(y, x + step, z))),
        ]

    def up_hops(s):
        return 4 if s % 2 == 0 else 3

    def ring_sends(s, p, away):
        ups = up_hops(s)
        go_up = away < ups
        go_down = (away == 0) | (away > ups + 1)
        return [
            (go_up, piece(s, p, z_send.at[s, p, 0], device(y, x, z + 1))),
            (go_down, piece(s, p, z_send.at[s, p, 1], device(y, x, z - 1))),
        ]

    def start(sends):
        for condition, copy in sends:
            pl.when(condition)(copy.start)

    def arrived(s, p):
        piece(s, p, z_send.at[s, p, 0], device(y, x, z + 1)).wait_recv()

    for s in range(LEAD_BLOCKS):

        @pl.when(z == s)
        def _(s=s):
            for p in range(len(pieces_of(s))):
                pl.when(jnp.logical_not(root))(lambda p=p: arrived(s, p))
                start(tree_sends(s, p))
                start(ring_sends(s, p, 0))

    def hop(t, carry):
        away = jnp.where(t % 2 == 1, (t + 1) // 2, Z - t // 2)
        for s in range(LEAD_BLOCKS):

            @pl.when(lax.rem(z - away + Z, Z) == s)
            def _(s=s):
                for p in range(len(pieces_of(s))):
                    arrived(s, p)
                    start(ring_sends(s, p, away))

        return carry

    lax.fori_loop(1, Z, hop, 0)

    for s in range(LEAD_BLOCKS):
        away = lax.rem(z - s + Z, Z)
        for p in range(len(pieces_of(s))):
            for condition, copy in ring_sends(s, p, away):
                pl.when(condition)(copy.wait_send)
            for condition, copy in tree_sends(s, p):
                pl.when(condition & (away == 0))(copy.wait_send)


def share(own):
    most = LEAD // PIECE
    return pl.pallas_call(
        share_kernel,
        out_shape=jax.ShapeDtypeStruct((LEAD_BLOCKS, BLOCK, LEAD), jnp.float32),
        in_specs=[ANY],
        out_specs=VMEM,
        scratch_shapes=[
            pltpu.SemaphoreType.DMA,
            pltpu.SemaphoreType.DMA((LEAD_BLOCKS, most, 2)),
            pltpu.SemaphoreType.DMA((most, 4)),
            pltpu.SemaphoreType.DMA((LEAD_BLOCKS, most)),
        ],
        compiler_params=pltpu.CompilerParams(
            collective_id=0, has_side_effects=True, vmem_limit_bytes=16 * MIB
        ),
        name="share",
    )(own)


def spread_out(x):
    return jnp.broadcast_to(x, (ROWS, BLOCK))


def refined_rsqrt(d):
    guess = lax.rsqrt(d)
    return guess * (1.5 - 0.5 * d * guess * guess)


def eliminate(parts, low, inv):
    done = []
    for r in range(ROWS):
        value = parts[r]
        for s in range(r):
            value = value - low[r][s] * done[s]
        done.append(value * inv[r])
    return done


def small_factor(cols):
    a = [[spread_out(cols[s][r : r + 1, :]) for s in range(r + 1)] for r in range(ROWS)]
    low = [[None] * ROWS for _ in range(ROWS)]
    inv = [None] * ROWS
    for s in range(ROWS):
        inv[s] = refined_rsqrt(a[s][s])
        for r in range(s + 1, ROWS):
            low[r][s] = a[r][s] * inv[s]
        for r in range(s + 1, ROWS):
            for t in range(s + 1, r + 1):
                a[r][t] = a[r][t] - low[r][s] * low[t][s]
    return low, inv


def invert_factor(a_ref, x_ref):
    row = lax.broadcasted_iota(jnp.int32, (BLOCK, BLOCK), 0)
    col = lax.broadcasted_iota(jnp.int32, (BLOCK, BLOCK), 1)
    x_ref[...] = jnp.where(row == col, 1.0, 0.0).astype(jnp.float32)
    for j in range(0, BLOCK, ROWS):
        w = a_ref[j : j + ROWS, :]
        e = x_ref[j : j + ROWS, :]
        low, inv = small_factor([spread_out(w[:, j + s : j + s + 1]) for s in range(ROWS)])
        y = eliminate([spread_out(w[r : r + 1, :]) for r in range(ROWS)], low, inv)
        f = eliminate([spread_out(e[r : r + 1, :]) for r in range(ROWS)], low, inv)
        for r in range(ROWS):
            x_ref[j + r : j + r + 1, :] = f[r][0:1, :]
        for i in range(j + ROWS, BLOCK, ROWS):
            block = a_ref[i : i + ROWS, :]
            other = x_ref[i : i + ROWS, :]
            z = eliminate(
                [spread_out(block[:, j + s : j + s + 1]) for s in range(ROWS)], low, inv
            )
            for s in range(ROWS):
                block = block - z[s] * y[s]
                other = other - z[s] * f[s]
            a_ref[i : i + ROWS, :] = block
            x_ref[i : i + ROWS, :] = other


def factor_kernel(index_ref, lead_ref, own_ref, l_ref, work, a_ref, x_ref):
    width = LEAD + BLOCK
    for s in range(LEAD_BLOCKS):
        work[s, :, 0:LEAD] = lead_ref[s]
        work[s, :, LEAD:width] = own_ref[:, s * BLOCK : (s + 1) * BLOCK].T
    per_panel = PANEL_WIDTH // BLOCK

    def step(b, carry):
        a_ref[...] = work[b, :, pl.ds(pl.multiple_of(b * BLOCK, BLOCK), BLOCK)]
        invert_factor(a_ref, x_ref)
        work[b] = dot(x_ref[...], work[b])

        def update(t, carry):
            crossing = work[b, :, pl.ds(pl.multiple_of(t * BLOCK, BLOCK), BLOCK)]
            work[t] = work[t] - dot(crossing, work[b], ((0,), (0,)))
            return carry

        lax.fori_loop(b + 1, (b // per_panel + 1) * per_panel, update, 0)

        @pl.when(b == per_panel - 1)
        def _():
            first = work[0:per_panel, :, PANEL_WIDTH:width].astype(jnp.bfloat16)
            first = first.reshape(PANEL_WIDTH, width - PANEL_WIDTH)
            for t in range(per_panel):
                rows = work[per_panel + t, :, PANEL_WIDTH:width]
                crossing = first[:, t * BLOCK : (t + 1) * BLOCK]
                work[per_panel + t, :, PANEL_WIDTH:width] = rows - dot(
                    crossing, first, ((0,), (0,)), None
                )

        return carry

    lax.fori_loop(0, LEAD_BLOCKS, step, 0)
    for s in range(LEAD_BLOCKS):
        q = lax.broadcasted_iota(jnp.int32, (BLOCK, BLOCK), 0) + s * BLOCK
        c = lax.broadcasted_iota(jnp.int32, (BLOCK, BLOCK), 1) + index_ref[0] * BLOCK
        own = jnp.where(q <= c, work[s, :, LEAD:width], 0.0)
        l_ref[:, s * BLOCK : (s + 1) * BLOCK] = own.T.astype(jnp.bfloat16)


def factor(index, lead, own):
    return pl.pallas_call(
        factor_kernel,
        out_shape=jax.ShapeDtypeStruct((BLOCK, LEAD), jnp.bfloat16),
        in_specs=[pl.BlockSpec(memory_space=pltpu.SMEM), VMEM, VMEM],
        out_specs=VMEM,
        scratch_shapes=[
            pltpu.VMEM((LEAD_BLOCKS, BLOCK, LEAD + BLOCK), jnp.float32),
            pltpu.VMEM((BLOCK, BLOCK), jnp.float32),
            pltpu.VMEM((BLOCK, BLOCK), jnp.float32),
        ],
        compiler_params=pltpu.CompilerParams(vmem_limit_bytes=32 * MIB),
        name="factor",
    )(index, lead, own)


STEPS = 2 * X


def exchange_kernel(
    l_ref, front_ref, tiles_ref, places_ref, index_ref, out_ref,
    line, plane, made, came, z_made, z_came, picked,
    local_sem, l_send, l_recv, p_send, p_recv, q_send, q_recv, z_send, z_recv,
):
    y, x, z = position()
    a = y * X + x
    up, down = device(y, x, z + 1), device(y, x, z - 1)
    right, left, over = device(y, x + 1, z), device(y, x - 1, z), device(1 - y, x, z)

    def plane_index(slot):
        return lax.rem(y + slot // X, 2) * X + lax.rem(x + lax.rem(slot, X), X)

    def plane_device(slot):
        return {"blk": plane_index(slot) * Z + z}

    greet([up, down] + [plane_device(slot) for slot in range(1, STEPS)])

    def rows(slot, half=None):
        if half is None:
            return pl.ds(slot * BLOCK, BLOCK)
        return pl.ds(slot * BLOCK + half * (BLOCK // 2), BLOCK // 2)

    own_line = pltpu.make_async_copy(l_ref, line.at[rows(0)], local_sem.at[0])
    own_plane = pltpu.make_async_copy(l_ref, plane.at[rows(0)], local_sem.at[1])
    base = pltpu.make_async_copy(front_ref, out_ref, local_sem.at[2])
    own_line.start()
    own_plane.start()
    base.start()

    def line_copy(way, hop):
        half = None if hop < Z // 2 else way
        sign = -1 if way == 0 else 1
        start, end = (sign * (hop - 1)) % Z, (sign * hop) % Z
        return remote(
            line.at[rows(start, half)],
            line.at[rows(end, half)],
            l_send.at[way, hop - 1],
            l_recv.at[way, hop - 1],
            up if way == 0 else down,
        )

    def plane_copy(number, start, end, half, target):
        return remote(
            plane.at[rows(start, half)],
            plane.at[rows(end, half)],
            p_send.at[number],
            p_recv.at[number],
            target,
        )

    across = [
        plane_copy(0, 0, 4, None, over),
        plane_copy(1, 0, 3, None, right),
        plane_copy(2, 0, 1, None, left),
        plane_copy(3, 4, 7, None, right),
        plane_copy(4, 4, 5, None, left),
        plane_copy(5, 3, 2, 0, right),
        plane_copy(6, 1, 2, 1, left),
        plane_copy(7, 7, 6, 0, right),
        plane_copy(8, 5, 6, 1, left),
    ]
    own_line.wait()
    line_copy(0, 1).start()
    line_copy(1, 1).start()
    own_plane.wait()
    for number in (0, 1, 2):
        across[number].start()

    slot_of = lax.broadcasted_iota(jnp.int32, (BLOCK, TILE_WIDTH), 0)
    column_table = jnp.where(slot_of == places_ref[...], 1.0, 0.0).astype(jnp.float32)
    order = picked.shape[1]
    for start in range(0, order, LEAD):
        picked[:, start : start + LEAD] = dot(column_table, tiles_ref[:, start : start + LEAD])
    pairs = order // BLOCK

    def place(pair, carry):
        start = lax.rem(pair + pairs // 2, pairs) * (2 * BLOCK)
        slot = lax.broadcasted_iota(jnp.int32, (2 * BLOCK, BLOCK), 0) + start
        row_table = jnp.where(slot == index_ref[pl.ds(pair, 1), :], 1.0, 0.0).astype(jnp.float32)
        part = picked[:, pl.ds(pl.multiple_of(pair * BLOCK, BLOCK), BLOCK)]
        columns = pl.ds(pl.multiple_of(start, BLOCK), 2 * BLOCK)
        out_ref[:, columns] = out_ref[:, columns] + dot(part, row_table, ((1,), (1,)))
        return carry

    def pass_on(hop):
        for way in (0, 1):
            line_copy(way, hop).wait_recv()
            line_copy(way, hop + 1).start()

    def pass_across(number, *onward):
        across[number].wait_recv()
        for other in onward:
            across[other].start()

    pass_on(1)
    pass_across(0, 3, 4)
    pass_across(1, 5)
    pass_across(2, 6)
    base.wait()
    lax.fori_loop(0, pairs // 4, place, 0)
    pass_on(2)
    pass_across(3, 7)
    pass_across(4, 8)
    lax.fori_loop(pairs // 4, pairs // 2, place, 0)
    pass_on(3)
    lax.fori_loop(pairs // 2, pairs, place, 0)
    for number in (5, 6, 7, 8):
        pass_across(number)
    for way in (0, 1):
        line_copy(way, Z // 2).wait_recv()

    def lefts(block, holder, zz):
        j = lax.broadcasted_iota(jnp.int32, (BLOCK, LEAD), 0) + lax.rem(zz + Z, Z) * BLOCK
        q = lax.broadcasted_iota(jnp.int32, (BLOCK, LEAD), 1)
        chosen = jnp.where(j == q, 1.0, 0.0).astype(jnp.bfloat16)
        is_lead = jnp.full((BLOCK, LEAD), holder, jnp.int32) == 0
        return jnp.where(is_lead, chosen, block)

    def product(left_side, right_side):
        return dot(left_side, right_side, ((1,), (1,)), None)

    near = (2 * BLOCK, 7 * BLOCK)

    def product_copy(slot):
        landing = slot // X * X + lax.rem(X - lax.rem(slot, X), X)
        return remote(
            made.at[slot], came.at[landing], q_send.at[slot], q_recv.at[landing], plane_device(slot)
        )

    def z_copy(way):
        return remote(
            z_made.at[way],
            z_came.at[way],
            z_send.at[way],
            z_recv.at[way],
            up if way == 0 else down,
        )

    sends = a != 0

    def make(slot, carry):
        block = plane[pl.ds(pl.multiple_of(slot * BLOCK, BLOCK), BLOCK)]
        made[slot] = product(lefts(block, plane_index(slot), z), line[near[0] : near[1]])

        @pl.when(sends & (slot > 1))
        def _():
            product_copy(slot - 1).start()

        return carry

    lax.fori_loop(1, STEPS, make, 0)
    z_made[0] = product(lefts(line[rows(1)], a, z + 1), plane[BLOCK:])
    pl.when(sends)(product_copy(STEPS - 1).start)
    z_made[1] = product(lefts(line[rows(Z - 1)], a, z - 1), plane[BLOCK:])
    z_copy(0).start()

    def put(aa, zz, value):
        block = aa * Z + lax.rem(zz + Z, Z)
        columns = pl.ds(pl.multiple_of(block * BLOCK, BLOCK), BLOCK)
        kept = jnp.where(jnp.full((BLOCK, BLOCK), aa, jnp.int32) == 0, 0.0, out_ref[:, columns] - value)
        is_lead = jnp.full((BLOCK, BLOCK), a, jnp.int32) == 0
        out_ref[:, columns] = jnp.where(is_lead, value, kept)

    own = lefts(line[rows(0)], a, z)
    along = product(own, line[...])
    z_copy(1).start()
    for s in range(Z):
        put(a, z + s, along[:, s * BLOCK : (s + 1) * BLOCK])
    along = product(own, plane[BLOCK:])
    for slot in range(1, STEPS):
        put(plane_index(slot), z, along[:, (slot - 1) * BLOCK : slot * BLOCK])
    for way in (0, 1):
        z_copy(way).wait_recv()
        for slot in range(1, STEPS):
            value = z_came[way, :, (slot - 1) * BLOCK : slot * BLOCK]
            put(plane_index(slot), z - 1 if way == 0 else z + 1, value)

    def take(slot, carry):
        source = plane_index(slot)

        @pl.when(source != 0)
        def _():
            landing = slot // X * X + lax.rem(X - lax.rem(slot, X), X)
            product_copy(landing).wait_recv()
            for s in range(2, Z - 1):
                put(source, z + s, came[slot, :, (s - 2) * BLOCK : (s - 1) * BLOCK])

        @pl.when(source == 0)
        def _():
            for s in range(2, Z - 1):
                columns = pl.ds(pl.multiple_of(lax.rem(z + s, Z) * BLOCK, BLOCK), BLOCK)
                out_ref[:, columns] = jnp.zeros((BLOCK, BLOCK), jnp.float32)

        return carry

    lax.fori_loop(1, STEPS, take, 0)
    for slot in range(1, STEPS):
        pl.when(sends)(product_copy(slot).wait_send)
    for way in (0, 1):
        z_copy(way).wait_send()
        for hop in range(1, Z // 2 + 1):
            line_copy(way, hop).wait_send()
    for copy in across:
        copy.wait_send()


def exchange(rows, front, tiles, places, index_map):
    dma = pltpu.SemaphoreType.DMA
    f32 = jnp.float32
    return pl.pallas_call(
        exchange_kernel,
        out_shape=jax.ShapeDtypeStruct(front.shape, f32),
        in_specs=[ANY, ANY, VMEM, VMEM, VMEM],
        out_specs=VMEM,
        scratch_shapes=[
            pltpu.VMEM((Z * BLOCK, LEAD), jnp.bfloat16),
            pltpu.VMEM((STEPS * BLOCK, LEAD), jnp.bfloat16),
            pltpu.VMEM((STEPS, BLOCK, 5 * BLOCK), f32),
            pltpu.VMEM((STEPS, BLOCK, 5 * BLOCK), f32),
            pltpu.VMEM((2, BLOCK, 7 * BLOCK), f32),
            pltpu.VMEM((2, BLOCK, 7 * BLOCK), f32),
            pltpu.VMEM((BLOCK, tiles.shape[1]), f32),
            dma((3,)),
            dma((2, Z // 2)),
            dma((2, Z // 2)),
            dma((9,)),
            dma((9,)),
            dma((STEPS,)),
            dma((STEPS,)),
            dma((2,)),
            dma((2,)),
        ],
        compiler_params=pltpu.CompilerParams(
            collective_id=1, has_side_effects=True, vmem_limit_bytes=40 * MIB
        ),
        name="exchange",
    )(rows, front, tiles, places, index_map)


def from_behind(shard, by):
    count = lax.axis_size("blk")
    return lax.ppermute(shard, "blk", [(i, (i + by) % count) for i in range(count)])


def contribution(tiles, places, own_places):
    slots = jnp.arange(BLOCK, dtype=jnp.int32)
    row_table = (places[..., None] == slots).astype(jnp.float32)
    shaped = tiles.reshape(TILE_WIDTH, -1, TILE_WIDTH)
    spread = jnp.einsum("cei,eiq->ceq", shaped, row_table, precision=HIGHEST)
    column_table = (own_places[..., None] == slots).astype(jnp.float32)
    return jnp.einsum(
        "cq,cn->qn", column_table, spread.reshape(TILE_WIDTH, -1), precision=HIGHEST
    )


def on_device(front, child, index_map):
    cycle = lax.axis_size("blk")
    half = cycle // 2
    index = lax.axis_index("blk")
    front, child = front[0], child[0]
    places = (index_map % BLOCK).reshape(cycle, TILE_WIDTH)
    own_places = lax.dynamic_index_in_dim(places, (index - half) % cycle, 0, keepdims=False)
    early = slice(half * TILE_WIDTH, (half + LEAD_BLOCKS) * TILE_WIDTH)
    early_tiles = from_behind(child[:, early], half)
    own = front[:, :LEAD] + contribution(
        early_tiles, places[half : half + LEAD_BLOCKS], own_places
    )
    lead = share(own)
    lead, child = lax.optimization_barrier((lead, child))
    tiles = from_behind(child, half)
    rows = factor(index[None].astype(jnp.int32), lead, own)
    return exchange(rows, front, tiles, own_places[None], index_map.reshape(-1, BLOCK))[None]


def solution(mesh):
    placed = (P("front", "blk", None), P("front", "blk", None), P("front"))
    return jax.shard_map(
        on_device, mesh=mesh, in_specs=placed, out_specs=P("front", "blk", None), check_vma=False
    )
```

```python
import jax
import jax.numpy as jnp
from jax import lax
from jax.experimental import pallas as pl
from jax.experimental.pallas import tpu as pltpu
from jax.sharding import PartitionSpec as P

PANEL_WIDTH = 512
BLOCK = 128
TILE_WIDTH = 64
LEAD = 2 * PANEL_WIDTH
LEAD_BLOCKS = LEAD // BLOCK
ROWS = 8
Z = 8
X = 4
PIECE = 256

HIGHEST = lax.Precision.HIGHEST
ANY = pl.BlockSpec(memory_space=pl.ANY)
VMEM = pl.BlockSpec(memory_space=pltpu.VMEM)
MIB = 1024 * 1024


def dot(a, b, dims=((1,), (0,)), precision=HIGHEST):
    return lax.dot_general(
        a, b, (dims, ((), ())), precision=precision, preferred_element_type=jnp.float32
    )


def position():
    me = lax.axis_index("blk")
    return me // (X * Z), me // Z % X, me % Z


def device(y, x, z):
    return {"blk": (y * X + lax.rem(x + X, X)) * Z + lax.rem(z + Z, Z)}


def remote(src, dst, send, recv, target):
    return pltpu.make_async_remote_copy(
        src_ref=src,
        dst_ref=dst,
        send_sem=send,
        recv_sem=recv,
        device_id=target,
        device_id_type=pl.DeviceIdType.MESH,
    )


def greet(partners):
    barrier = pltpu.get_barrier_semaphore()
    for partner in partners:
        pl.semaphore_signal(
            barrier, inc=1, device_id=partner, device_id_type=pl.DeviceIdType.MESH
        )
    pl.semaphore_wait(barrier, len(partners))


def spread_out(x):
    return jnp.broadcast_to(x, (ROWS, BLOCK))


def refined_rsqrt(d):
    guess = lax.rsqrt(d)
    return guess * (1.5 - 0.5 * d * guess * guess)


def eliminate(parts, low, inv):
    done = []
    for r in range(ROWS):
        value = parts[r]
        for s in range(r):
            value = value - low[r][s] * done[s]
        done.append(value * inv[r])
    return done


def small_factor(cols):
    a = [[spread_out(cols[s][r : r + 1, :]) for s in range(r + 1)] for r in range(ROWS)]
    low = [[None] * ROWS for _ in range(ROWS)]
    inv = [None] * ROWS
    for s in range(ROWS):
        inv[s] = refined_rsqrt(a[s][s])
        for r in range(s + 1, ROWS):
            low[r][s] = a[r][s] * inv[s]
        for r in range(s + 1, ROWS):
            for t in range(s + 1, r + 1):
                a[r][t] = a[r][t] - low[r][s] * low[t][s]
    return low, inv


def invert_factor(a_ref, x_ref):
    row = lax.broadcasted_iota(jnp.int32, (BLOCK, BLOCK), 0)
    col = lax.broadcasted_iota(jnp.int32, (BLOCK, BLOCK), 1)
    x_ref[...] = jnp.where(row == col, 1.0, 0.0).astype(jnp.float32)
    for j in range(0, BLOCK, ROWS):
        w = a_ref[j : j + ROWS, :]
        e = x_ref[j : j + ROWS, :]
        low, inv = small_factor([spread_out(w[:, j + s : j + s + 1]) for s in range(ROWS)])
        y = eliminate([spread_out(w[r : r + 1, :]) for r in range(ROWS)], low, inv)
        f = eliminate([spread_out(e[r : r + 1, :]) for r in range(ROWS)], low, inv)
        for r in range(ROWS):
            x_ref[j + r : j + r + 1, :] = f[r][0:1, :]
        for i in range(j + ROWS, BLOCK, ROWS):
            block = a_ref[i : i + ROWS, :]
            other = x_ref[i : i + ROWS, :]
            z = eliminate(
                [spread_out(block[:, j + s : j + s + 1]) for s in range(ROWS)], low, inv
            )
            for s in range(ROWS):
                block = block - z[s] * y[s]
                other = other - z[s] * f[s]
            a_ref[i : i + ROWS, :] = block
            x_ref[i : i + ROWS, :] = other


PANEL_BLOCKS = PANEL_WIDTH // BLOCK
WIDTH = PANEL_WIDTH + BLOCK


def pieces_of(s, first):
    edges = [s * BLOCK] + [c for c in range(PIECE, LEAD + 1, PIECE) if c > s * BLOCK]
    spans = zip(edges[:-1], edges[1:])
    return [((c1 - 1) // PIECE, c0, c1) for c0, c1 in spans if (c1 <= PANEL_WIDTH) == first]


def factor_kernel(
    own_ref, child_ref, l_ref, tiles_ref, lead, work, a_ref, x_ref, inverses,
    local_sem, z_send, a_send, recv, tile_sem,
):
    y, x, z = position()
    over = device(1 - y, x, z)
    right, left = device(y, x + 1, z), device(y, x - 1, z)
    up, down = device(y, x, z + 1), device(y, x, z - 1)
    greet([over, right, left, up, down])
    root = (y == 0) & (x == 0)

    def piece(s, span, send, target):
        p, c0, c1 = span
        part = lead.at[s, :, c0:c1]
        return remote(part, part, send, recv.at[s, p], target)

    def tree_sends(s, span):
        p = span[0]
        onward = (x == 1) if p % 2 == 0 else (x == 3)
        return [
            (root, piece(s, span, a_send.at[p, 0], over)),
            (x == 0, piece(s, span, a_send.at[p, 1], right)),
            (x == 0, piece(s, span, a_send.at[p, 2], left)),
            (onward, piece(s, span, a_send.at[p, 3], right if p % 2 == 0 else left)),
        ]

    def ring_sends(s, span, away):
        p = span[0]
        ups = Z // 2 if s % 2 == 0 else Z // 2 - 1
        go_up = away < ups
        go_down = (away == 0) | (away > ups + 1)
        return [
            (go_up, piece(s, span, z_send.at[s, p, 0], up)),
            (go_down, piece(s, span, z_send.at[s, p, 1], down)),
        ]

    def start(sends):
        for condition, copy in sends:
            pl.when(condition)(copy.start)

    def arrived(s, span):
        piece(s, span, z_send.at[s, span[0], 0], up).wait_recv()

    def each_slab(slab, first, act):
        for s in range(LEAD_BLOCKS):
            spans = pieces_of(s, first)
            if spans:

                @pl.when(slab == s)
                def _(s=s, spans=spans):
                    for span in spans:
                        act(s, span)

    def tree(first):
        def act(s, span):
            pl.when(jnp.logical_not(root))(lambda: arrived(s, span))
            start(tree_sends(s, span))
            if first:
                start(ring_sends(s, span, 0))

        each_slab(z, first, act)

    def hop(t, first):
        away = jnp.where(lax.rem(t, 2) == 1, (t + 1) // 2, Z - t // 2)

        def act(s, span):
            arrived(s, span)
            start(ring_sends(s, span, away))

        each_slab(lax.rem(z - away + Z, Z), first, act)

    @pl.when(root)
    def _():
        copy = pltpu.make_async_copy(own_ref, lead.at[z], local_sem)
        copy.start()
        copy.wait()

    tree(True)
    level = y + jnp.where(x == 0, 0, 1) + jnp.where(x == 2, 1, 0)
    turn = jnp.where(level == 0, 1, jnp.where(level == 1, 3, jnp.where(level == 2, 6, 8)))
    for s in range(LEAD_BLOCKS):
        own_part = own_ref[:, s * BLOCK : (s + 1) * BLOCK].T
        work[s, :, PANEL_WIDTH:WIDTH] = own_part

    def first_hops(t, carry):
        pl.when(t == turn)(lambda: tree(False))
        pl.when(t < Z)(lambda: hop(t, True))
        return carry

    lax.fori_loop(1, Z + 1, first_hops, 0)
    each_slab(z, False, lambda s, span: start(ring_sends(s, span, 0)))
    for s in range(PANEL_BLOCKS):
        work[s, :, 0:PANEL_WIDTH] = lead[s, :, 0:PANEL_WIDTH]

    tiles_copy = remote(child_ref, tiles_ref, tile_sem.at[0], tile_sem.at[1], over)

    def step(b, carry):
        panel = b // PANEL_BLOCKS
        window = pl.ds(pl.multiple_of(panel * PANEL_WIDTH, BLOCK), WIDTH)

        def block(t):
            return pl.ds(pl.multiple_of((t + panel) * BLOCK, BLOCK), BLOCK)

        @pl.when((b > 0) & (b < PANEL_BLOCKS))
        def _():
            def act(t, carry):
                hop(t, False)
                return carry

            lax.fori_loop(2 * b - 1, 2 * b + 1, act, 0)

        pl.when(b == PANEL_BLOCKS)(tiles_copy.start)
        a_ref[...] = work[b, :, block(b)]
        invert_factor(a_ref, x_ref)
        inverses[b] = x_ref[...]
        work[b, :, window] = dot(x_ref[...], work[b, :, window])

        def update(t, carry):
            crossing = work[b, :, block(t)]
            work[t, :, window] = work[t, :, window] - dot(crossing, work[b, :, window], ((0,), (0,)))
            return carry

        lax.fori_loop(b + 1, (panel + 1) * PANEL_BLOCKS, update, 0)

        @pl.when(b == PANEL_BLOCKS - 1)
        def _():
            hop(jnp.full((), Z - 1, jnp.int32), False)
            for s in range(LEAD_BLOCKS):
                work[s, :, WIDTH:] = lead[s, :, PANEL_WIDTH:LEAD]

            def solve(s, carry):
                work[s, :, WIDTH:] = dot(inverses[s], work[s, :, WIDTH:])

                def update(t, carry):
                    crossing = work[s, :, pl.ds(pl.multiple_of(t * BLOCK, BLOCK), BLOCK)]
                    rest = dot(crossing, work[s, :, WIDTH:], ((0,), (0,)))
                    work[t, :, WIDTH:] = work[t, :, WIDTH:] - rest
                    return carry

                lax.fori_loop(s + 1, PANEL_BLOCKS, update, 0)
                return carry

            lax.fori_loop(0, PANEL_BLOCKS, solve, 0)
            first = work[0:PANEL_BLOCKS, :, PANEL_WIDTH:].astype(jnp.bfloat16)
            first = first.reshape(PANEL_WIDTH, WIDTH)
            for t in range(PANEL_BLOCKS):
                rows = work[PANEL_BLOCKS + t, :, PANEL_WIDTH:]
                crossing = first[:, (t + 1) * BLOCK : (t + 2) * BLOCK]
                work[PANEL_BLOCKS + t, :, PANEL_WIDTH:] = rows - dot(
                    crossing, first, ((0,), (0,)), None
                )

        return carry

    lax.fori_loop(0, LEAD_BLOCKS, step, 0)
    mine = ((y * X + x) * Z + z) * BLOCK
    for s in range(LEAD_BLOCKS):
        q = lax.broadcasted_iota(jnp.int32, (BLOCK, BLOCK), 0) + s * BLOCK
        c = lax.broadcasted_iota(jnp.int32, (BLOCK, BLOCK), 1) + mine
        own = jnp.where(q <= c, work[s, :, PANEL_WIDTH:WIDTH], 0.0)
        l_ref[:, s * BLOCK : (s + 1) * BLOCK] = own.T.astype(jnp.bfloat16)

    tiles_copy.wait()
    for s in range(LEAD_BLOCKS):
        away = lax.rem(z - s + Z, Z)
        for span in pieces_of(s, True) + pieces_of(s, False):
            for condition, copy in ring_sends(s, span, away):
                pl.when(condition)(copy.wait_send)
            for condition, copy in tree_sends(s, span):
                pl.when(condition & (away == 0))(copy.wait_send)


def factor(own, child):
    dma = pltpu.SemaphoreType.DMA
    f32 = jnp.float32
    return pl.pallas_call(
        factor_kernel,
        out_shape=[
            jax.ShapeDtypeStruct((BLOCK, LEAD), jnp.bfloat16),
            jax.ShapeDtypeStruct(child.shape, f32),
        ],
        in_specs=[VMEM, ANY],
        out_specs=[VMEM, VMEM],
        scratch_shapes=[
            pltpu.VMEM((LEAD_BLOCKS, BLOCK, LEAD), f32),
            pltpu.VMEM((LEAD_BLOCKS, BLOCK, LEAD + BLOCK), f32),
            pltpu.VMEM((BLOCK, BLOCK), f32),
            pltpu.VMEM((BLOCK, BLOCK), f32),
            pltpu.VMEM((LEAD_BLOCKS, BLOCK, BLOCK), f32),
            dma,
            dma((LEAD_BLOCKS, LEAD // PIECE, 2)),
            dma((LEAD // PIECE, 4)),
            dma((LEAD_BLOCKS, LEAD // PIECE)),
            dma((2,)),
        ],
        compiler_params=pltpu.CompilerParams(
            collective_id=0, has_side_effects=True, vmem_limit_bytes=32 * MIB
        ),
        name="factor",
    )(own, child)


STEPS = 2 * X


def exchange_kernel(
    l_ref, front_ref, tiles_ref, places_ref, index_ref, out_ref,
    line, plane, made, came, z_made, z_came, picked,
    local_sem, l_send, l_recv, p_send, p_recv, q_send, q_recv, z_send, z_recv,
):
    y, x, z = position()
    a = y * X + x
    up, down = device(y, x, z + 1), device(y, x, z - 1)
    right, left, over = device(y, x + 1, z), device(y, x - 1, z), device(1 - y, x, z)

    def plane_index(slot):
        return lax.rem(y + slot // X, 2) * X + lax.rem(x + lax.rem(slot, X), X)

    def plane_device(slot):
        return {"blk": plane_index(slot) * Z + z}

    greet([up, down] + [plane_device(slot) for slot in range(1, STEPS)])

    def rows(slot, half=None):
        if half is None:
            return pl.ds(slot * BLOCK, BLOCK)
        return pl.ds(slot * BLOCK + half * (BLOCK // 2), BLOCK // 2)

    own_line = pltpu.make_async_copy(l_ref, line.at[rows(0)], local_sem.at[0])
    own_plane = pltpu.make_async_copy(l_ref, plane.at[rows(0)], local_sem.at[1])
    base = pltpu.make_async_copy(front_ref, out_ref, local_sem.at[2])
    own_line.start()
    own_plane.start()
    base.start()

    def line_copy(way, hop):
        half = None if hop < Z // 2 else way
        sign = -1 if way == 0 else 1
        start, end = (sign * (hop - 1)) % Z, (sign * hop) % Z
        return remote(
            line.at[rows(start, half)],
            line.at[rows(end, half)],
            l_send.at[way, hop - 1],
            l_recv.at[way, hop - 1],
            up if way == 0 else down,
        )

    def plane_copy(number, start, end, half, target):
        return remote(
            plane.at[rows(start, half)],
            plane.at[rows(end, half)],
            p_send.at[number],
            p_recv.at[number],
            target,
        )

    across = [
        plane_copy(0, 0, 4, None, over),
        plane_copy(1, 0, 3, None, right),
        plane_copy(2, 0, 1, None, left),
        plane_copy(3, 4, 7, None, right),
        plane_copy(4, 4, 5, None, left),
        plane_copy(5, 3, 2, 0, right),
        plane_copy(6, 1, 2, 1, left),
        plane_copy(7, 7, 6, 0, right),
        plane_copy(8, 5, 6, 1, left),
    ]
    own_line.wait()
    line_copy(0, 1).start()
    line_copy(1, 1).start()
    own_plane.wait()
    for number in (0, 1, 2):
        across[number].start()

    slot_of = lax.broadcasted_iota(jnp.int32, (BLOCK, TILE_WIDTH), 0)
    column_table = jnp.where(slot_of == places_ref[...], 1.0, 0.0).astype(jnp.float32)
    order = picked.shape[1]
    for start in range(0, order, LEAD):
        picked[:, start : start + LEAD] = dot(column_table, tiles_ref[:, start : start + LEAD])
    pairs = order // BLOCK

    def place(pair, carry):
        start = lax.rem(pair + pairs // 2, pairs) * (2 * BLOCK)
        slot = lax.broadcasted_iota(jnp.int32, (2 * BLOCK, BLOCK), 0) + start
        row_table = jnp.where(slot == index_ref[pl.ds(pair, 1), :], 1.0, 0.0).astype(jnp.float32)
        part = picked[:, pl.ds(pl.multiple_of(pair * BLOCK, BLOCK), BLOCK)]
        columns = pl.ds(pl.multiple_of(start, BLOCK), 2 * BLOCK)
        out_ref[:, columns] = out_ref[:, columns] + dot(part, row_table, ((1,), (1,)))
        return carry

    def pass_on(hop):
        for way in (0, 1):
            line_copy(way, hop).wait_recv()
            line_copy(way, hop + 1).start()

    def pass_across(number, *onward):
        across[number].wait_recv()
        for other in onward:
            across[other].start()

    pass_on(1)
    pass_across(0, 3, 4)
    pass_across(1, 5)
    pass_across(2, 6)
    base.wait()
    lax.fori_loop(0, pairs // 4, place, 0)
    pass_on(2)
    pass_across(3, 7)
    pass_across(4, 8)
    lax.fori_loop(pairs // 4, pairs // 2, place, 0)
    pass_on(3)
    lax.fori_loop(pairs // 2, pairs, place, 0)
    for number in (5, 6, 7, 8):
        pass_across(number)
    for way in (0, 1):
        line_copy(way, Z // 2).wait_recv()

    def lefts(block, holder, zz):
        j = lax.broadcasted_iota(jnp.int32, (BLOCK, LEAD), 0) + lax.rem(zz + Z, Z) * BLOCK
        q = lax.broadcasted_iota(jnp.int32, (BLOCK, LEAD), 1)
        chosen = jnp.where(j == q, 1.0, 0.0).astype(jnp.bfloat16)
        is_lead = jnp.full((BLOCK, LEAD), holder, jnp.int32) == 0
        return jnp.where(is_lead, chosen, block)

    def product(left_side, right_side):
        return dot(left_side, right_side, ((1,), (1,)), None)

    near = (2 * BLOCK, 7 * BLOCK)

    def product_copy(slot):
        landing = slot // X * X + lax.rem(X - lax.rem(slot, X), X)
        return remote(
            made.at[slot], came.at[landing], q_send.at[slot], q_recv.at[landing], plane_device(slot)
        )

    def z_copy(way):
        return remote(
            z_made.at[way],
            z_came.at[way],
            z_send.at[way],
            z_recv.at[way],
            up if way == 0 else down,
        )

    sends = a != 0

    def make(slot, carry):
        block = plane[pl.ds(pl.multiple_of(slot * BLOCK, BLOCK), BLOCK)]
        made[slot] = product(lefts(block, plane_index(slot), z), line[near[0] : near[1]])

        @pl.when(sends & (slot > 1))
        def _():
            product_copy(slot - 1).start()

        return carry

    lax.fori_loop(1, STEPS, make, 0)
    z_made[0] = product(lefts(line[rows(1)], a, z + 1), plane[BLOCK:])
    pl.when(sends)(product_copy(STEPS - 1).start)
    z_made[1] = product(lefts(line[rows(Z - 1)], a, z - 1), plane[BLOCK:])
    z_copy(0).start()

    def put(aa, zz, value):
        block = aa * Z + lax.rem(zz + Z, Z)
        columns = pl.ds(pl.multiple_of(block * BLOCK, BLOCK), BLOCK)
        kept = jnp.where(jnp.full((BLOCK, BLOCK), aa, jnp.int32) == 0, 0.0, out_ref[:, columns] - value)
        is_lead = jnp.full((BLOCK, BLOCK), a, jnp.int32) == 0
        out_ref[:, columns] = jnp.where(is_lead, value, kept)

    own = lefts(line[rows(0)], a, z)
    along = product(own, line[...])
    z_copy(1).start()
    for s in range(Z):
        put(a, z + s, along[:, s * BLOCK : (s + 1) * BLOCK])
    along = product(own, plane[BLOCK:])
    for slot in range(1, STEPS):
        put(plane_index(slot), z, along[:, (slot - 1) * BLOCK : slot * BLOCK])
    for way in (0, 1):
        z_copy(way).wait_recv()
        for slot in range(1, STEPS):
            value = z_came[way, :, (slot - 1) * BLOCK : slot * BLOCK]
            put(plane_index(slot), z - 1 if way == 0 else z + 1, value)

    def take(slot, carry):
        source = plane_index(slot)

        @pl.when(source != 0)
        def _():
            landing = slot // X * X + lax.rem(X - lax.rem(slot, X), X)
            product_copy(landing).wait_recv()
            for s in range(2, Z - 1):
                put(source, z + s, came[slot, :, (s - 2) * BLOCK : (s - 1) * BLOCK])

        @pl.when(source == 0)
        def _():
            for s in range(2, Z - 1):
                columns = pl.ds(pl.multiple_of(lax.rem(z + s, Z) * BLOCK, BLOCK), BLOCK)
                out_ref[:, columns] = jnp.zeros((BLOCK, BLOCK), jnp.float32)

        return carry

    lax.fori_loop(1, STEPS, take, 0)
    for slot in range(1, STEPS):
        pl.when(sends)(product_copy(slot).wait_send)
    for way in (0, 1):
        z_copy(way).wait_send()
        for hop in range(1, Z // 2 + 1):
            line_copy(way, hop).wait_send()
    for copy in across:
        copy.wait_send()


def exchange(rows, front, tiles, places, index_map):
    dma = pltpu.SemaphoreType.DMA
    f32 = jnp.float32
    return pl.pallas_call(
        exchange_kernel,
        out_shape=jax.ShapeDtypeStruct(front.shape, f32),
        in_specs=[ANY, ANY, VMEM, VMEM, VMEM],
        out_specs=VMEM,
        scratch_shapes=[
            pltpu.VMEM((Z * BLOCK, LEAD), jnp.bfloat16),
            pltpu.VMEM((STEPS * BLOCK, LEAD), jnp.bfloat16),
            pltpu.VMEM((STEPS, BLOCK, 5 * BLOCK), f32),
            pltpu.VMEM((STEPS, BLOCK, 5 * BLOCK), f32),
            pltpu.VMEM((2, BLOCK, 7 * BLOCK), f32),
            pltpu.VMEM((2, BLOCK, 7 * BLOCK), f32),
            pltpu.VMEM((BLOCK, tiles.shape[1]), f32),
            dma((3,)),
            dma((2, Z // 2)),
            dma((2, Z // 2)),
            dma((9,)),
            dma((9,)),
            dma((STEPS,)),
            dma((STEPS,)),
            dma((2,)),
            dma((2,)),
        ],
        compiler_params=pltpu.CompilerParams(
            collective_id=1, has_side_effects=True, vmem_limit_bytes=40 * MIB
        ),
        name="exchange",
    )(rows, front, tiles, places, index_map)


def from_behind(shard, by):
    count = lax.axis_size("blk")
    return lax.ppermute(shard, "blk", [(i, (i + by) % count) for i in range(count)])


def contribution(tiles, places, own_places):
    slots = jnp.arange(BLOCK, dtype=jnp.int32)
    row_table = (places[..., None] == slots).astype(jnp.float32)
    shaped = tiles.reshape(TILE_WIDTH, -1, TILE_WIDTH)
    spread = jnp.einsum("cei,eiq->ceq", shaped, row_table, precision=HIGHEST)
    column_table = (own_places[..., None] == slots).astype(jnp.float32)
    return jnp.einsum(
        "cq,cn->qn", column_table, spread.reshape(TILE_WIDTH, -1), precision=HIGHEST
    )


def on_device(front, child, index_map):
    cycle = lax.axis_size("blk")
    half = cycle // 2
    index = lax.axis_index("blk")
    front, child = front[0], child[0]
    places = (index_map % BLOCK).reshape(cycle, TILE_WIDTH)
    own_places = lax.dynamic_index_in_dim(places, (index - half) % cycle, 0, keepdims=False)
    early = slice(half * TILE_WIDTH, (half + LEAD_BLOCKS) * TILE_WIDTH)
    early_tiles = from_behind(child[:, early], half)
    own = front[:, :LEAD] + contribution(
        early_tiles, places[half : half + LEAD_BLOCKS], own_places
    )
    rows, tiles = factor(own, child)
    return exchange(rows, front, tiles, own_places[None], index_map.reshape(-1, BLOCK))[None]


def solution(mesh):
    placed = (P("front", "blk", None), P("front", "blk", None), P("front"))
    return jax.shard_map(
        on_device, mesh=mesh, in_specs=placed, out_specs=P("front", "blk", None), check_vma=False
    )
```

```python
import jax
import jax.numpy as jnp
from jax import lax
from jax.experimental import pallas as pl
from jax.experimental.pallas import tpu as pltpu
from jax.sharding import PartitionSpec as P

PANEL_WIDTH = 512
BLOCK = 128
TILE_WIDTH = 64
LEAD = 2 * PANEL_WIDTH
LEAD_BLOCKS = LEAD // BLOCK
ROWS = 8
Z = 8
X = 4
PIECE = 128

HIGHEST = lax.Precision.HIGHEST
VMEM = pl.BlockSpec(memory_space=pltpu.VMEM)
HBM = pl.BlockSpec(memory_space=pltpu.HBM)
MIB = 1024 * 1024


def dot(a, b, dims=((1,), (0,)), precision=HIGHEST):
    return lax.dot_general(
        a, b, (dims, ((), ())), precision=precision, preferred_element_type=jnp.float32
    )


def position():
    me = lax.axis_index("blk")
    return me // (X * Z), me // Z % X, me % Z


def device(y, x, z):
    return {"blk": (y * X + lax.rem(x + X, X)) * Z + lax.rem(z + Z, Z)}


def remote(src, dst, send, recv, target):
    return pltpu.make_async_remote_copy(
        src_ref=src,
        dst_ref=dst,
        send_sem=send,
        recv_sem=recv,
        device_id=target,
        device_id_type=pl.DeviceIdType.MESH,
    )


def greet(partners):
    barrier = pltpu.get_barrier_semaphore()
    for partner in partners:
        pl.semaphore_signal(
            barrier, inc=1, device_id=partner, device_id_type=pl.DeviceIdType.MESH
        )
    pl.semaphore_wait(barrier, len(partners))


def spread_out(x):
    return jnp.broadcast_to(x, (ROWS, BLOCK))


def eliminate(parts, low, inv):
    done = []
    for r in range(ROWS):
        value = parts[r]
        for s in range(r):
            value = value - low[r][s] * done[s]
        done.append(value * inv[r])
    return done


def small_factor(cols):
    a = [[spread_out(cols[s][r : r + 1, :]) for s in range(r + 1)] for r in range(ROWS)]
    low = [[None] * ROWS for _ in range(ROWS)]
    inv = [None] * ROWS
    for s in range(ROWS):
        inv[s] = lax.rsqrt(a[s][s])
        for r in range(s + 1, ROWS):
            low[r][s] = a[r][s] * inv[s]
        for r in range(s + 1, ROWS):
            for t in range(s + 1, r + 1):
                a[r][t] = a[r][t] - low[r][s] * low[t][s]
    return low, inv


def invert_factor(a_ref, x_ref):
    row = lax.broadcasted_iota(jnp.int32, (BLOCK, BLOCK), 0)
    col = lax.broadcasted_iota(jnp.int32, (BLOCK, BLOCK), 1)
    x_ref[...] = jnp.where(row == col, 1.0, 0.0).astype(jnp.float32)
    for j in range(0, BLOCK, ROWS):
        w = a_ref[j : j + ROWS, :]
        e = x_ref[j : j + ROWS, :]
        low, inv = small_factor([spread_out(w[:, j + s : j + s + 1]) for s in range(ROWS)])
        y = eliminate([spread_out(w[r : r + 1, :]) for r in range(ROWS)], low, inv)
        f = eliminate([spread_out(e[r : r + 1, :]) for r in range(ROWS)], low, inv)
        for r in range(ROWS):
            x_ref[j + r : j + r + 1, :] = f[r][0:1, :]
        for i in range(j + ROWS, BLOCK, ROWS):
            block = a_ref[i : i + ROWS, :]
            other = x_ref[i : i + ROWS, :]
            z = eliminate(
                [spread_out(block[:, j + s : j + s + 1]) for s in range(ROWS)], low, inv
            )
            for s in range(ROWS):
                block = block - z[s] * y[s]
                other = other - z[s] * f[s]
            a_ref[i : i + ROWS, :] = block
            x_ref[i : i + ROWS, :] = other


PANEL_BLOCKS = PANEL_WIDTH // BLOCK
WIDTH = PANEL_WIDTH + BLOCK


def pieces_of(s, first):
    edges = [s * BLOCK] + [c for c in range(PIECE, LEAD + 1, PIECE) if c > s * BLOCK]
    spans = zip(edges[:-1], edges[1:])
    return [((c1 - 1) // PIECE, c0, c1) for c0, c1 in spans if (c1 <= PANEL_WIDTH) == first]


STEPS = 2 * X


def front_kernel(
    own_ref, child_ref, front_ref, places_ref, index_ref, out_ref,
    lead, work, a_ref, x_ref, inverses, tiles, staged,
    line, plane, made, came, z_made, z_came, picked,
    local_sem, b_send, a_send, b_recv, tile_sem, own_sem,
    l_send, l_recv, p_send, p_recv, q_send, q_recv, z_send, z_recv,
):
    y, x, z = position()
    a = y * X + x
    over = device(1 - y, x, z)
    right, left = device(y, x + 1, z), device(y, x - 1, z)
    up, down = device(y, x, z + 1), device(y, x, z - 1)

    def plane_index(slot):
        return lax.rem(y + slot // X, 2) * X + lax.rem(x + lax.rem(slot, X), X)

    def plane_device(slot):
        return {"blk": plane_index(slot) * Z + z}

    greet([up, down] + [plane_device(slot) for slot in range(1, STEPS)])
    base = pltpu.make_async_copy(front_ref, out_ref, local_sem.at[1])
    base.start()
    root = a == 0

    def rows(slot, half=None):
        if half is None:
            return pl.ds(slot * BLOCK, BLOCK)
        return pl.ds(slot * BLOCK + half * (BLOCK // 2), BLOCK // 2)

    def panel_columns(panel):
        return pl.ds(panel * PANEL_WIDTH, PANEL_WIDTH)

    def own_copies(panel):
        return [
            pltpu.make_async_copy(
                staged.at[panel], target.at[rows(0), panel_columns(panel)], own_sem.at[panel, i]
            )
            for i, target in enumerate((line, plane))
        ]

    def keep_rows(panel):
        for i in range(PANEL_BLOCKS):
            s = panel * PANEL_BLOCKS + i
            q = lax.broadcasted_iota(jnp.int32, (BLOCK, BLOCK), 0) + s * BLOCK
            c = lax.broadcasted_iota(jnp.int32, (BLOCK, BLOCK), 1) + (a * Z + z) * BLOCK
            own = jnp.where(q <= c, work[s, :, PANEL_WIDTH:WIDTH], 0.0)
            staged[panel, :, i * BLOCK : (i + 1) * BLOCK] = own.T.astype(jnp.bfloat16)
        for copy in own_copies(panel):
            copy.start()

    def line_copy(panel, way, hop):
        half = None if hop < Z // 2 else way
        sign = -1 if way == 0 else 1
        start, end = (sign * (hop - 1)) % Z, (sign * hop) % Z
        return remote(
            line.at[rows(start, half), panel_columns(panel)],
            line.at[rows(end, half), panel_columns(panel)],
            l_send.at[panel, way, hop - 1],
            l_recv.at[panel, way, hop - 1],
            up if way == 0 else down,
        )

    def across(panel, number):
        start, end, half, target = [
            (0, 4, None, over),
            (0, 3, None, right),
            (0, 1, None, left),
            (4, 7, None, right),
            (4, 5, None, left),
            (3, 2, 0, right),
            (1, 2, 1, left),
            (7, 6, 0, right),
            (5, 6, 1, left),
        ][number]
        return remote(
            plane.at[rows(start, half), panel_columns(panel)],
            plane.at[rows(end, half), panel_columns(panel)],
            p_send.at[panel, number],
            p_recv.at[panel, number],
            target,
        )

    def gather(panel):
        along, beside = own_copies(panel)
        along.wait()
        line_copy(panel, 0, 1).start()
        line_copy(panel, 1, 1).start()
        beside.wait()
        for number in (0, 1, 2):
            across(panel, number).start()

    def pass_on(panel, hop):
        for way in (0, 1):
            line_copy(panel, way, hop).wait_recv()
            line_copy(panel, way, hop + 1).start()

    def pass_across(panel, number, *onward):
        across(panel, number).wait_recv()
        for other in onward:
            across(panel, other).start()

    def gather_first(panel):
        pass_on(panel, 1)
        pass_across(panel, 0, 3, 4)
        pass_across(panel, 1, 5)
        pass_across(panel, 2, 6)

    def gather_second(panel):
        pass_on(panel, 2)
        pass_across(panel, 3, 7)
        pass_across(panel, 4, 8)

    def gather_third(panel):
        pass_on(panel, 3)

    def gather_last(panel):
        for number in (5, 6, 7, 8):
            across(panel, number).wait_recv()
        for way in (0, 1):
            line_copy(panel, way, Z // 2).wait_recv()

    def piece(s, span, send, target):
        p, c0, c1 = span
        part = lead.at[s, :, c0:c1]
        return remote(part, part, send, b_recv.at[s, p], target)

    def tree_sends(s, span):
        p = span[0]
        onward = (x == 1) if p % 2 == 0 else (x == 3)
        return [
            (root, piece(s, span, a_send.at[p, 0], over)),
            (x == 0, piece(s, span, a_send.at[p, 1], right)),
            (x == 0, piece(s, span, a_send.at[p, 2], left)),
            (onward, piece(s, span, a_send.at[p, 3], right if p % 2 == 0 else left)),
        ]

    def ring_sends(s, span, away):
        p = span[0]
        ups = Z // 2 if s % 2 == 0 else Z // 2 - 1
        go_up = away < ups
        go_down = (away == 0) | (away > ups + 1)
        return [
            (go_up, piece(s, span, b_send.at[s, p, 0], up)),
            (go_down, piece(s, span, b_send.at[s, p, 1], down)),
        ]

    def start(sends):
        for condition, copy in sends:
            pl.when(condition)(copy.start)

    def arrived(s, span):
        piece(s, span, b_send.at[s, span[0], 0], up).wait_recv()

    def each_slab(slab, first, act):
        for s in range(LEAD_BLOCKS):
            spans = pieces_of(s, first)
            if spans:

                @pl.when(slab == s)
                def _(s=s, spans=spans):
                    for span in spans:
                        act(s, span)

    def tree(first):
        def act(s, span):
            pl.when(jnp.logical_not(root))(lambda: arrived(s, span))
            start(tree_sends(s, span))
            if first:
                start(ring_sends(s, span, 0))

        each_slab(z, first, act)

    def hop(t, first):
        away = jnp.where(lax.rem(t, 2) == 1, (t + 1) // 2, Z - t // 2)

        def act(s, span):
            arrived(s, span)
            start(ring_sends(s, span, away))

        each_slab(lax.rem(z - away + Z, Z), first, act)

    @pl.when(root)
    def _():
        copy = pltpu.make_async_copy(own_ref, lead.at[z], local_sem.at[0])
        copy.start()
        copy.wait()

    tree(True)
    level = y + jnp.where(x == 0, 0, 1) + jnp.where(x == 2, 1, 0)
    turn = jnp.where(level == 0, 1, jnp.where(level == 1, 3, jnp.where(level == 2, 6, 8)))
    for s in range(LEAD_BLOCKS):
        own_part = own_ref[:, s * BLOCK : (s + 1) * BLOCK].T
        work[s, :, PANEL_WIDTH:WIDTH] = own_part

    def first_hops(t, carry):
        pl.when(t == turn)(lambda: tree(False))
        pl.when(t < Z)(lambda: hop(t, True))
        return carry

    lax.fori_loop(1, Z + 1, first_hops, 0)
    each_slab(z, False, lambda s, span: start(ring_sends(s, span, 0)))
    for s in range(PANEL_BLOCKS):
        work[s, :, 0:PANEL_WIDTH] = lead[s, :, 0:PANEL_WIDTH]

    tiles_copy = remote(child_ref, tiles, tile_sem.at[0], tile_sem.at[1], over)

    def step(b, carry):
        panel = b // PANEL_BLOCKS
        window = pl.ds(pl.multiple_of(panel * PANEL_WIDTH, BLOCK), WIDTH)

        def block(t):
            return pl.ds(pl.multiple_of((t + panel) * BLOCK, BLOCK), BLOCK)

        @pl.when((b > 0) & (b < PANEL_BLOCKS))
        def _():
            def act(t, carry):
                hop(t, False)
                return carry

            lax.fori_loop(2 * b - 1, 2 * b + 1, act, 0)

        pl.when(b == 2)(tiles_copy.start)
        pl.when(b == PANEL_BLOCKS + 1)(lambda: gather_first(0))
        pl.when(b == PANEL_BLOCKS + 2)(lambda: gather_third(0))
        a_ref[...] = work[b, :, block(b)]
        invert_factor(a_ref, x_ref)
        inverses[b] = x_ref[...]
        pl.when(b == PANEL_BLOCKS)(lambda: gather(0))
        pl.when(b == PANEL_BLOCKS + 1)(lambda: gather_second(0))
        work[b, :, window] = dot(x_ref[...], work[b, :, window])

        def update(t, carry):
            crossing = work[b, :, block(t)]
            work[t, :, window] = work[t, :, window] - dot(crossing, work[b, :, window], ((0,), (0,)))
            return carry

        lax.fori_loop(b + 1, (panel + 1) * PANEL_BLOCKS, update, 0)

        @pl.when(b == PANEL_BLOCKS - 1)
        def _():
            hop(jnp.full((), Z - 1, jnp.int32), False)
            for s in range(LEAD_BLOCKS):
                work[s, :, WIDTH:] = lead[s, :, PANEL_WIDTH:LEAD]

            def solve(s, carry):
                work[s, :, WIDTH:] = dot(inverses[s], work[s, :, WIDTH:])

                def update(t, carry):
                    crossing = work[s, :, pl.ds(pl.multiple_of(t * BLOCK, BLOCK), BLOCK)]
                    rest = dot(crossing, work[s, :, WIDTH:], ((0,), (0,)))
                    work[t, :, WIDTH:] = work[t, :, WIDTH:] - rest
                    return carry

                lax.fori_loop(s + 1, PANEL_BLOCKS, update, 0)
                return carry

            lax.fori_loop(0, PANEL_BLOCKS, solve, 0)
            first = work[0:PANEL_BLOCKS, :, PANEL_WIDTH:].astype(jnp.bfloat16)
            first = first.reshape(PANEL_WIDTH, WIDTH)
            for t in range(PANEL_BLOCKS):
                rows = work[PANEL_BLOCKS + t, :, PANEL_WIDTH:]
                crossing = first[:, (t + 1) * BLOCK : (t + 2) * BLOCK]
                work[PANEL_BLOCKS + t, :, PANEL_WIDTH:] = rows - dot(
                    crossing, first, ((0,), (0,)), None
                )
            keep_rows(0)

        return carry

    lax.fori_loop(0, LEAD_BLOCKS, step, 0)
    keep_rows(1)
    gather(1)
    tiles_copy.wait_recv()

    slot_of = lax.broadcasted_iota(jnp.int32, (BLOCK, TILE_WIDTH), 0)
    column_table = jnp.where(slot_of == places_ref[...], 1.0, 0.0).astype(jnp.float32)
    order = picked.shape[1]
    for start in range(0, order, LEAD):
        picked[:, start : start + LEAD] = dot(column_table, tiles[:, start : start + LEAD])
    pairs = order // BLOCK

    def place(pair, carry):
        start = lax.rem(pair + pairs // 2, pairs) * (2 * BLOCK)
        slot = lax.broadcasted_iota(jnp.int32, (2 * BLOCK, BLOCK), 0) + start
        row_table = jnp.where(slot == index_ref[pl.ds(pair, 1), :], 1.0, 0.0).astype(jnp.float32)
        part = picked[:, pl.ds(pl.multiple_of(pair * BLOCK, BLOCK), BLOCK)]
        columns = pl.ds(pl.multiple_of(start, BLOCK), 2 * BLOCK)
        out_ref[:, columns] = out_ref[:, columns] + dot(part, row_table, ((1,), (1,)))
        return carry

    gather_first(1)
    base.wait()
    lax.fori_loop(0, pairs // 4, place, 0)
    gather_second(1)
    lax.fori_loop(pairs // 4, pairs // 2, place, 0)
    gather_third(1)
    lax.fori_loop(pairs // 2, pairs, place, 0)
    gather_last(0)
    gather_last(1)

    def lefts(block, holder, zz):
        j = lax.broadcasted_iota(jnp.int32, (BLOCK, LEAD), 0) + lax.rem(zz + Z, Z) * BLOCK
        q = lax.broadcasted_iota(jnp.int32, (BLOCK, LEAD), 1)
        chosen = jnp.where(j == q, 1.0, 0.0).astype(jnp.bfloat16)
        is_lead = jnp.full((BLOCK, LEAD), holder, jnp.int32) == 0
        return jnp.where(is_lead, chosen, block)

    def product(left_side, right_side):
        return dot(left_side, right_side, ((1,), (1,)), None)

    near = (2 * BLOCK, 7 * BLOCK)

    def product_copy(slot):
        landing = slot // X * X + lax.rem(X - lax.rem(slot, X), X)
        return remote(
            made.at[slot], came.at[landing], q_send.at[slot], q_recv.at[landing], plane_device(slot)
        )

    def z_copy(way):
        return remote(
            z_made.at[way],
            z_came.at[way],
            z_send.at[way],
            z_recv.at[way],
            up if way == 0 else down,
        )

    sends = a != 0

    def make(slot, carry):
        block = plane[pl.ds(pl.multiple_of(slot * BLOCK, BLOCK), BLOCK)]
        made[slot] = product(lefts(block, plane_index(slot), z), line[near[0] : near[1]])

        @pl.when(sends & (slot > 1))
        def _():
            product_copy(slot - 1).start()

        return carry

    lax.fori_loop(1, STEPS, make, 0)
    z_made[0] = product(lefts(line[rows(1)], a, z + 1), plane[BLOCK:])
    pl.when(sends)(product_copy(STEPS - 1).start)
    z_made[1] = product(lefts(line[rows(Z - 1)], a, z - 1), plane[BLOCK:])
    z_copy(0).start()

    def put(aa, zz, value):
        block = aa * Z + lax.rem(zz + Z, Z)
        columns = pl.ds(pl.multiple_of(block * BLOCK, BLOCK), BLOCK)
        kept = jnp.where(jnp.full((BLOCK, BLOCK), aa, jnp.int32) == 0, 0.0, out_ref[:, columns] - value)
        is_lead = jnp.full((BLOCK, BLOCK), a, jnp.int32) == 0
        out_ref[:, columns] = jnp.where(is_lead, value, kept)

    own = lefts(line[rows(0)], a, z)
    along = product(own, line[...])
    z_copy(1).start()
    for s in range(Z):
        put(a, z + s, along[:, s * BLOCK : (s + 1) * BLOCK])
    along = product(own, plane[BLOCK:])
    for slot in range(1, STEPS):
        put(plane_index(slot), z, along[:, (slot - 1) * BLOCK : slot * BLOCK])
    for way in (0, 1):
        z_copy(way).wait_recv()
        for slot in range(1, STEPS):
            value = z_came[way, :, (slot - 1) * BLOCK : slot * BLOCK]
            put(plane_index(slot), z - 1 if way == 0 else z + 1, value)

    def take(slot, carry):
        source = plane_index(slot)

        @pl.when(source != 0)
        def _():
            landing = slot // X * X + lax.rem(X - lax.rem(slot, X), X)
            product_copy(landing).wait_recv()
            for s in range(2, Z - 1):
                put(source, z + s, came[slot, :, (s - 2) * BLOCK : (s - 1) * BLOCK])

        @pl.when(source == 0)
        def _():
            for s in range(2, Z - 1):
                columns = pl.ds(pl.multiple_of(lax.rem(z + s, Z) * BLOCK, BLOCK), BLOCK)
                out_ref[:, columns] = jnp.zeros((BLOCK, BLOCK), jnp.float32)

        return carry

    lax.fori_loop(1, STEPS, take, 0)
    for slot in range(1, STEPS):
        pl.when(sends)(product_copy(slot).wait_send)
    for way in (0, 1):
        z_copy(way).wait_send()
    tiles_copy.wait_send()
    for panel in (0, 1):
        for way in (0, 1):
            for hop_number in range(1, Z // 2 + 1):
                line_copy(panel, way, hop_number).wait_send()
        for number in range(9):
            across(panel, number).wait_send()
    for s in range(LEAD_BLOCKS):
        away = lax.rem(z - s + Z, Z)
        for span in pieces_of(s, True) + pieces_of(s, False):
            for condition, copy in ring_sends(s, span, away):
                pl.when(condition)(copy.wait_send)
            for condition, copy in tree_sends(s, span):
                pl.when(condition & (away == 0))(copy.wait_send)


def whole(own, child, front, places, index_map):
    dma = pltpu.SemaphoreType.DMA
    f32, bf16 = jnp.float32, jnp.bfloat16
    return pl.pallas_call(
        front_kernel,
        out_shape=jax.ShapeDtypeStruct(front.shape, f32),
        in_specs=[VMEM, HBM, HBM, VMEM, VMEM],
        out_specs=VMEM,
        scratch_shapes=[
            pltpu.VMEM((LEAD_BLOCKS, BLOCK, LEAD), f32),
            pltpu.VMEM((LEAD_BLOCKS, BLOCK, LEAD + BLOCK), f32),
            pltpu.VMEM((BLOCK, BLOCK), f32),
            pltpu.VMEM((BLOCK, BLOCK), f32),
            pltpu.VMEM((LEAD_BLOCKS, BLOCK, BLOCK), f32),
            pltpu.VMEM(child.shape, f32),
            pltpu.VMEM((2, BLOCK, PANEL_WIDTH), bf16),
            pltpu.VMEM((Z * BLOCK, LEAD), bf16),
            pltpu.VMEM((STEPS * BLOCK, LEAD), bf16),
            pltpu.VMEM((STEPS, BLOCK, 5 * BLOCK), f32),
            pltpu.VMEM((STEPS, BLOCK, 5 * BLOCK), f32),
            pltpu.VMEM((2, BLOCK, 7 * BLOCK), f32),
            pltpu.VMEM((2, BLOCK, 7 * BLOCK), f32),
            pltpu.VMEM((BLOCK, child.shape[1]), f32),
            dma((2,)),
            dma((LEAD_BLOCKS, LEAD // PIECE, 2)),
            dma((LEAD // PIECE, 4)),
            dma((LEAD_BLOCKS, LEAD // PIECE)),
            dma((2,)),
            dma((2, 2)),
            dma((2, 2, Z // 2)),
            dma((2, 2, Z // 2)),
            dma((2, 9)),
            dma((2, 9)),
            dma((STEPS,)),
            dma((STEPS,)),
            dma((2,)),
            dma((2,)),
        ],
        compiler_params=pltpu.CompilerParams(
            collective_id=0, has_side_effects=True, vmem_limit_bytes=48 * MIB
        ),
        name="front",
    )(own, child, front, places, index_map)


def from_behind(shard, by):
    count = lax.axis_size("blk")
    return lax.ppermute(shard, "blk", [(i, (i + by) % count) for i in range(count)])


def contribution(tiles, places, own_places):
    slots = jnp.arange(BLOCK, dtype=jnp.int32)
    row_table = (places[..., None] == slots).astype(jnp.float32)
    shaped = tiles.reshape(TILE_WIDTH, -1, TILE_WIDTH)
    spread = jnp.einsum("cei,eiq->ceq", shaped, row_table, precision=HIGHEST)
    column_table = (own_places[..., None] == slots).astype(jnp.float32)
    return jnp.einsum(
        "cq,cn->qn", column_table, spread.reshape(TILE_WIDTH, -1), precision=HIGHEST
    )


def on_device(front, child, index_map):
    cycle = lax.axis_size("blk")
    half = cycle // 2
    index = lax.axis_index("blk")
    front, child = front[0], child[0]
    places = (index_map % BLOCK).reshape(cycle, TILE_WIDTH)
    own_places = lax.dynamic_index_in_dim(places, (index - half) % cycle, 0, keepdims=False)
    early = slice(half * TILE_WIDTH, (half + LEAD_BLOCKS) * TILE_WIDTH)
    early_tiles = from_behind(child[:, early], half)
    own = front[:, :LEAD] + contribution(
        early_tiles, places[half : half + LEAD_BLOCKS], own_places
    )
    return whole(own, child, front, own_places[None], index_map.reshape(-1, BLOCK))[None]


def solution(mesh):
    placed = (P("front", "blk", None), P("front", "blk", None), P("front"))
    return jax.shard_map(
        on_device, mesh=mesh, in_specs=placed, out_specs=P("front", "blk", None), check_vma=False
    )
```

```python
import jax
import jax.numpy as jnp
from jax import lax
from jax.experimental import pallas as pl
from jax.experimental.pallas import tpu as pltpu
from jax.sharding import PartitionSpec as P

PANEL_WIDTH = 512
BLOCK = 128
TILE_WIDTH = 64
LEAD = 2 * PANEL_WIDTH
LEAD_BLOCKS = LEAD // BLOCK
ROWS = 8
Z = 8
X = 4
PIECE = 128

HIGHEST = lax.Precision.HIGHEST
VMEM = pl.BlockSpec(memory_space=pltpu.VMEM)
HBM = pl.BlockSpec(memory_space=pltpu.HBM)
MIB = 1024 * 1024


def dot(a, b, dims=((1,), (0,)), precision=HIGHEST):
    return lax.dot_general(
        a, b, (dims, ((), ())), precision=precision, preferred_element_type=jnp.float32
    )


def position():
    me = lax.axis_index("blk")
    return me // (X * Z), me // Z % X, me % Z


def device(y, x, z):
    return {"blk": (y * X + lax.rem(x + X, X)) * Z + lax.rem(z + Z, Z)}


def remote(src, dst, send, recv, target):
    return pltpu.make_async_remote_copy(
        src_ref=src,
        dst_ref=dst,
        send_sem=send,
        recv_sem=recv,
        device_id=target,
        device_id_type=pl.DeviceIdType.MESH,
    )


def greet(partners):
    barrier = pltpu.get_barrier_semaphore()
    for partner in partners:
        pl.semaphore_signal(
            barrier, inc=1, device_id=partner, device_id_type=pl.DeviceIdType.MESH
        )
    pl.semaphore_wait(barrier, len(partners))


def spread_out(x):
    return jnp.broadcast_to(x, (ROWS, BLOCK))


def eliminate(parts, low, inv):
    done = []
    for r in range(ROWS):
        value = parts[r]
        for s in range(r):
            value = value - low[r][s] * done[s]
        done.append(value * inv[r])
    return done


def small_factor(cols):
    a = [[spread_out(cols[s][r : r + 1, :]) for s in range(r + 1)] for r in range(ROWS)]
    low = [[None] * ROWS for _ in range(ROWS)]
    inv = [None] * ROWS
    for s in range(ROWS):
        inv[s] = lax.rsqrt(a[s][s])
        for r in range(s + 1, ROWS):
            low[r][s] = a[r][s] * inv[s]
        for r in range(s + 1, ROWS):
            for t in range(s + 1, r + 1):
                a[r][t] = a[r][t] - low[r][s] * low[t][s]
    return low, inv


def invert_factor(a_ref, x_ref):
    row = lax.broadcasted_iota(jnp.int32, (BLOCK, BLOCK), 0)
    col = lax.broadcasted_iota(jnp.int32, (BLOCK, BLOCK), 1)
    x_ref[...] = jnp.where(row == col, 1.0, 0.0).astype(jnp.float32)
    for j in range(0, BLOCK, ROWS):
        w = a_ref[j : j + ROWS, :]
        e = x_ref[j : j + ROWS, :]
        low, inv = small_factor([spread_out(w[:, j + s : j + s + 1]) for s in range(ROWS)])
        y = eliminate([spread_out(w[r : r + 1, :]) for r in range(ROWS)], low, inv)
        f = eliminate([spread_out(e[r : r + 1, :]) for r in range(ROWS)], low, inv)
        for r in range(ROWS):
            x_ref[j + r : j + r + 1, :] = f[r][0:1, :]
        for i in range(j + ROWS, BLOCK, ROWS):
            block = a_ref[i : i + ROWS, :]
            other = x_ref[i : i + ROWS, :]
            z = eliminate(
                [spread_out(block[:, j + s : j + s + 1]) for s in range(ROWS)], low, inv
            )
            for s in range(ROWS):
                block = block - z[s] * y[s]
                other = other - z[s] * f[s]
            a_ref[i : i + ROWS, :] = block
            x_ref[i : i + ROWS, :] = other


PANEL_BLOCKS = PANEL_WIDTH // BLOCK
WIDTH = PANEL_WIDTH + BLOCK


def pieces_of(s, first):
    edges = [s * BLOCK] + [c for c in range(PIECE, LEAD + 1, PIECE) if c > s * BLOCK]
    spans = zip(edges[:-1], edges[1:])
    return [((c1 - 1) // PIECE, c0, c1) for c0, c1 in spans if (c1 <= PANEL_WIDTH) == first]


STEPS = 2 * X


def front_kernel(
    own_ref, child_ref, front_ref, places_ref, index_ref, out_ref,
    lead, work, a_ref, x_ref, inverses, tiles, staged,
    line, plane, made, came, z_made, z_came, two_made, two_came, picked,
    local_sem, b_send, a_send, b_recv, tile_sem, own_sem,
    l_send, l_recv, p_send, p_recv, q_send, q_recv, z_send, z_recv, two_send, two_recv,
):
    y, x, z = position()
    a = y * X + x
    over = device(1 - y, x, z)
    right, left = device(y, x + 1, z), device(y, x - 1, z)
    up, down = device(y, x, z + 1), device(y, x, z - 1)

    def plane_index(slot):
        return lax.rem(y + slot // X, 2) * X + lax.rem(x + lax.rem(slot, X), X)

    def plane_device(slot):
        return {"blk": plane_index(slot) * Z + z}

    up_two, down_two = device(y, x, z + 2), device(y, x, z - 2)
    greet([up, down, up_two, down_two] + [plane_device(slot) for slot in range(1, STEPS)])
    base = pltpu.make_async_copy(front_ref, out_ref, local_sem.at[1])
    base.start()
    root = a == 0

    def rows(slot, half=None):
        if half is None:
            return pl.ds(slot * BLOCK, BLOCK)
        return pl.ds(slot * BLOCK + half * (BLOCK // 2), BLOCK // 2)

    def panel_columns(panel):
        return pl.ds(panel * PANEL_WIDTH, PANEL_WIDTH)

    def own_copies(panel):
        return [
            pltpu.make_async_copy(
                staged.at[panel], target.at[rows(0), panel_columns(panel)], own_sem.at[panel, i]
            )
            for i, target in enumerate((line, plane))
        ]

    def keep_rows(panel):
        for i in range(PANEL_BLOCKS):
            s = panel * PANEL_BLOCKS + i
            q = lax.broadcasted_iota(jnp.int32, (BLOCK, BLOCK), 0) + s * BLOCK
            c = lax.broadcasted_iota(jnp.int32, (BLOCK, BLOCK), 1) + (a * Z + z) * BLOCK
            own = jnp.where(q <= c, work[s, :, PANEL_WIDTH:WIDTH], 0.0)
            staged[panel, :, i * BLOCK : (i + 1) * BLOCK] = own.T.astype(jnp.bfloat16)
        for copy in own_copies(panel):
            copy.start()

    def line_copy(panel, way, hop):
        half = None if hop < Z // 2 else way
        sign = -1 if way == 0 else 1
        start, end = (sign * (hop - 1)) % Z, (sign * hop) % Z
        return remote(
            line.at[rows(start, half), panel_columns(panel)],
            line.at[rows(end, half), panel_columns(panel)],
            l_send.at[panel, way, hop - 1],
            l_recv.at[panel, way, hop - 1],
            up if way == 0 else down,
        )

    def across(panel, number):
        start, end, half, target = [
            (0, 4, None, over),
            (0, 3, None, right),
            (0, 1, None, left),
            (4, 7, None, right),
            (4, 5, None, left),
            (3, 2, 0, right),
            (1, 2, 1, left),
            (7, 6, 0, right),
            (5, 6, 1, left),
        ][number]
        return remote(
            plane.at[rows(start, half), panel_columns(panel)],
            plane.at[rows(end, half), panel_columns(panel)],
            p_send.at[panel, number],
            p_recv.at[panel, number],
            target,
        )

    def gather(panel):
        along, beside = own_copies(panel)
        along.wait()
        line_copy(panel, 0, 1).start()
        line_copy(panel, 1, 1).start()
        beside.wait()
        for number in (0, 1, 2):
            across(panel, number).start()

    def pass_on(panel, hop):
        for way in (0, 1):
            line_copy(panel, way, hop).wait_recv()
            line_copy(panel, way, hop + 1).start()

    def pass_across(panel, number, *onward):
        across(panel, number).wait_recv()
        for other in onward:
            across(panel, other).start()

    def gather_first(panel):
        pass_on(panel, 1)
        pass_across(panel, 0, 3, 4)
        pass_across(panel, 1, 5)
        pass_across(panel, 2, 6)

    def gather_second(panel):
        pass_on(panel, 2)
        pass_across(panel, 3, 7)
        pass_across(panel, 4, 8)

    def gather_third(panel):
        pass_on(panel, 3)

    def gather_last(panel):
        for number in (5, 6, 7, 8):
            across(panel, number).wait_recv()
        for way in (0, 1):
            line_copy(panel, way, Z // 2).wait_recv()

    def piece(s, span, send, target):
        p, c0, c1 = span
        part = lead.at[s, :, c0:c1]
        return remote(part, part, send, b_recv.at[s, p], target)

    def tree_sends(s, span):
        p = span[0]
        onward = (x == 1) if p % 2 == 0 else (x == 3)
        return [
            (root, piece(s, span, a_send.at[p, 0], over)),
            (x == 0, piece(s, span, a_send.at[p, 1], right)),
            (x == 0, piece(s, span, a_send.at[p, 2], left)),
            (onward, piece(s, span, a_send.at[p, 3], right if p % 2 == 0 else left)),
        ]

    def ring_sends(s, span, away):
        p = span[0]
        ups = Z // 2 if s % 2 == 0 else Z // 2 - 1
        go_up = away < ups
        go_down = (away == 0) | (away > ups + 1)
        return [
            (go_up, piece(s, span, b_send.at[s, p, 0], up)),
            (go_down, piece(s, span, b_send.at[s, p, 1], down)),
        ]

    def start(sends):
        for condition, copy in sends:
            pl.when(condition)(copy.start)

    def arrived(s, span):
        piece(s, span, b_send.at[s, span[0], 0], up).wait_recv()

    def each_slab(slab, first, act):
        for s in range(LEAD_BLOCKS):
            spans = pieces_of(s, first)
            if spans:

                @pl.when(slab == s)
                def _(s=s, spans=spans):
                    for span in spans:
                        act(s, span)

    def tree(first):
        def act(s, span):
            pl.when(jnp.logical_not(root))(lambda: arrived(s, span))
            start(tree_sends(s, span))
            if first:
                start(ring_sends(s, span, 0))

        each_slab(z, first, act)

    def hop(t, first):
        away = jnp.where(lax.rem(t, 2) == 1, (t + 1) // 2, Z - t // 2)

        def act(s, span):
            arrived(s, span)
            start(ring_sends(s, span, away))

        each_slab(lax.rem(z - away + Z, Z), first, act)

    @pl.when(root)
    def _():
        copy = pltpu.make_async_copy(own_ref, lead.at[z], local_sem.at[0])
        copy.start()
        copy.wait()

    tree(True)
    level = y + jnp.where(x == 0, 0, 1) + jnp.where(x == 2, 1, 0)
    turn = jnp.where(level == 0, 1, jnp.where(level == 1, 3, jnp.where(level == 2, 6, 8)))
    for s in range(LEAD_BLOCKS):
        own_part = own_ref[:, s * BLOCK : (s + 1) * BLOCK].T
        work[s, :, PANEL_WIDTH:WIDTH] = own_part

    def first_hops(t, carry):
        pl.when(t == turn)(lambda: tree(False))
        pl.when(t < Z)(lambda: hop(t, True))
        return carry

    lax.fori_loop(1, Z + 1, first_hops, 0)
    each_slab(z, False, lambda s, span: start(ring_sends(s, span, 0)))
    for s in range(PANEL_BLOCKS):
        work[s, :, 0:PANEL_WIDTH] = lead[s, :, 0:PANEL_WIDTH]

    tiles_copy = remote(child_ref, tiles, tile_sem.at[0], tile_sem.at[1], over)

    def step(b, carry):
        panel = b // PANEL_BLOCKS
        window = pl.ds(pl.multiple_of(panel * PANEL_WIDTH, BLOCK), WIDTH)

        def block(t):
            return pl.ds(pl.multiple_of((t + panel) * BLOCK, BLOCK), BLOCK)

        @pl.when((b > 0) & (b < PANEL_BLOCKS))
        def _():
            def act(t, carry):
                hop(t, False)
                return carry

            lax.fori_loop(2 * b - 1, 2 * b + 1, act, 0)

        pl.when(b == 2)(tiles_copy.start)
        pl.when(b == PANEL_BLOCKS + 1)(lambda: gather_first(0))
        pl.when(b == PANEL_BLOCKS + 2)(lambda: gather_third(0))
        a_ref[...] = work[b, :, block(b)]
        invert_factor(a_ref, x_ref)
        inverses[b] = x_ref[...]
        pl.when(b == PANEL_BLOCKS)(lambda: gather(0))
        pl.when(b == PANEL_BLOCKS + 1)(lambda: gather_second(0))
        work[b, :, window] = dot(x_ref[...], work[b, :, window])

        def update(t, carry):
            crossing = work[b, :, block(t)]
            work[t, :, window] = work[t, :, window] - dot(crossing, work[b, :, window], ((0,), (0,)))
            return carry

        lax.fori_loop(b + 1, (panel + 1) * PANEL_BLOCKS, update, 0)

        @pl.when(b == PANEL_BLOCKS - 1)
        def _():
            hop(jnp.full((), Z - 1, jnp.int32), False)
            for s in range(LEAD_BLOCKS):
                work[s, :, WIDTH:] = lead[s, :, PANEL_WIDTH:LEAD]

            def solve(s, carry):
                work[s, :, WIDTH:] = dot(inverses[s], work[s, :, WIDTH:])

                def update(t, carry):
                    crossing = work[s, :, pl.ds(pl.multiple_of(t * BLOCK, BLOCK), BLOCK)]
                    rest = dot(crossing, work[s, :, WIDTH:], ((0,), (0,)))
                    work[t, :, WIDTH:] = work[t, :, WIDTH:] - rest
                    return carry

                lax.fori_loop(s + 1, PANEL_BLOCKS, update, 0)
                return carry

            lax.fori_loop(0, PANEL_BLOCKS, solve, 0)
            first = work[0:PANEL_BLOCKS, :, PANEL_WIDTH:].astype(jnp.bfloat16)
            first = first.reshape(PANEL_WIDTH, WIDTH)
            for t in range(PANEL_BLOCKS):
                rows = work[PANEL_BLOCKS + t, :, PANEL_WIDTH:]
                crossing = first[:, (t + 1) * BLOCK : (t + 2) * BLOCK]
                work[PANEL_BLOCKS + t, :, PANEL_WIDTH:] = rows - dot(
                    crossing, first, ((0,), (0,)), None
                )
            keep_rows(0)

        return carry

    lax.fori_loop(0, LEAD_BLOCKS, step, 0)
    keep_rows(1)
    gather(1)
    gather_first(1)
    gather_second(1)
    gather_third(1)
    gather_last(0)
    gather_last(1)

    def lefts(block, holder, zz):
        j = lax.broadcasted_iota(jnp.int32, (BLOCK, LEAD), 0) + lax.rem(zz + Z, Z) * BLOCK
        q = lax.broadcasted_iota(jnp.int32, (BLOCK, LEAD), 1)
        chosen = jnp.where(j == q, 1.0, 0.0).astype(jnp.bfloat16)
        is_lead = jnp.full((BLOCK, LEAD), holder, jnp.int32) == 0
        return jnp.where(is_lead, chosen, block)

    def product(left_side, right_side):
        return dot(left_side, right_side, ((1,), (1,)), None)

    def first_of(slot):
        return jnp.where(slot < X, 2, 3)

    def product_copy(slot):
        landing = slot // X * X + lax.rem(X - lax.rem(slot, X), X)
        return remote(
            made.at[slot], came.at[landing], q_send.at[slot], q_recv.at[landing], plane_device(slot)
        )

    def z_copy(way):
        return remote(
            z_made.at[way],
            z_came.at[way],
            z_send.at[way],
            z_recv.at[way],
            up if way == 0 else down,
        )

    two_slots = (range(1, X), range(X, STEPS))

    def two_copy(way):
        width = len(two_slots[way]) * BLOCK
        return remote(
            two_made.at[way, :, 0:width],
            two_came.at[way, :, 0:width],
            two_send.at[way],
            two_recv.at[way],
            up_two if way == 0 else down_two,
        )

    sends = a != 0

    def slot_at(i):
        return lax.rem(i * 5, STEPS)

    def make(i, carry):
        slot = slot_at(i)
        block = plane[pl.ds(pl.multiple_of(slot * BLOCK, BLOCK), BLOCK)]
        part = line[pl.ds(pl.multiple_of(first_of(slot) * BLOCK, BLOCK), 4 * BLOCK)]
        made[slot] = product(lefts(block, plane_index(slot), z), part)

        @pl.when(sends & (i > 1))
        def _():
            product_copy(slot_at(i - 1)).start()

        return carry

    lax.fori_loop(1, STEPS, make, 0)
    two_made[0, :, 0 : (X - 1) * BLOCK] = product(
        lefts(line[rows(2)], a, z + 2), plane[BLOCK : X * BLOCK]
    )
    pl.when(sends)(product_copy(slot_at(jnp.full((), STEPS - 1, jnp.int32))).start)
    two_made[1] = product(lefts(line[rows(Z - 2)], a, z - 2), plane[X * BLOCK :])
    two_copy(0).start()
    z_made[0] = product(lefts(line[rows(1)], a, z + 1), plane[BLOCK:])
    two_copy(1).start()
    z_made[1] = product(lefts(line[rows(Z - 1)], a, z - 1), plane[BLOCK:])
    z_copy(0).start()

    def put(aa, zz, value):
        block = aa * Z + lax.rem(zz + Z, Z)
        columns = pl.ds(pl.multiple_of(block * BLOCK, BLOCK), BLOCK)
        kept = jnp.where(jnp.full((BLOCK, BLOCK), aa, jnp.int32) == 0, 0.0, out_ref[:, columns] - value)
        is_lead = jnp.full((BLOCK, BLOCK), a, jnp.int32) == 0
        out_ref[:, columns] = jnp.where(is_lead, value, kept)

    own = lefts(line[rows(0)], a, z)
    along = product(own, line[...])
    z_copy(1).start()
    base.wait()
    tiles_copy.wait_recv()
    slot_of = lax.broadcasted_iota(jnp.int32, (BLOCK, TILE_WIDTH), 0)
    column_table = jnp.where(slot_of == places_ref[...], 1.0, 0.0).astype(jnp.float32)
    order = picked.shape[1]
    for start in range(0, order, LEAD):
        picked[:, start : start + LEAD] = dot(column_table, tiles[:, start : start + LEAD])
    pairs = order // BLOCK

    def place(pair, carry):
        start = lax.rem(pair + pairs // 2, pairs) * (2 * BLOCK)
        slot = lax.broadcasted_iota(jnp.int32, (2 * BLOCK, BLOCK), 0) + start
        row_table = jnp.where(slot == index_ref[pl.ds(pair, 1), :], 1.0, 0.0).astype(jnp.float32)
        part = picked[:, pl.ds(pl.multiple_of(pair * BLOCK, BLOCK), BLOCK)]
        columns = pl.ds(pl.multiple_of(start, BLOCK), 2 * BLOCK)
        out_ref[:, columns] = out_ref[:, columns] + dot(part, row_table, ((1,), (1,)))
        return carry

    lax.fori_loop(0, pairs, place, 0)
    for s in range(Z):
        put(a, z + s, along[:, s * BLOCK : (s + 1) * BLOCK])
    along = product(own, plane[BLOCK:])
    for slot in range(1, STEPS):
        put(plane_index(slot), z, along[:, (slot - 1) * BLOCK : slot * BLOCK])
    for way in (0, 1):
        z_copy(way).wait_recv()
        for slot in range(1, STEPS):
            value = z_came[way, :, (slot - 1) * BLOCK : slot * BLOCK]
            put(plane_index(slot), z - 1 if way == 0 else z + 1, value)
    for way in (0, 1):
        two_copy(way).wait_recv()
        for i, slot in enumerate(two_slots[way]):
            value = two_came[way, :, i * BLOCK : (i + 1) * BLOCK]
            put(plane_index(slot), z - 2 if way == 0 else z + 2, value)

    def take(i, carry):
        slot = slot_at(i)
        source = plane_index(slot)

        @pl.when(source != 0)
        def _():
            landing = slot // X * X + lax.rem(X - lax.rem(slot, X), X)
            product_copy(landing).wait_recv()
            for s in range(4):
                value = came[slot, :, s * BLOCK : (s + 1) * BLOCK]
                put(source, z + first_of(slot) + s, value)

        @pl.when(source == 0)
        def _():
            for s in range(4):
                zz = lax.rem(z + first_of(slot) + s, Z)
                columns = pl.ds(pl.multiple_of(zz * BLOCK, BLOCK), BLOCK)
                out_ref[:, columns] = jnp.zeros((BLOCK, BLOCK), jnp.float32)

        return carry

    lax.fori_loop(1, STEPS, take, 0)
    for slot in range(1, STEPS):
        pl.when(sends)(product_copy(slot).wait_send)
    for way in (0, 1):
        z_copy(way).wait_send()
        two_copy(way).wait_send()
    tiles_copy.wait_send()
    for panel in (0, 1):
        for way in (0, 1):
            for hop_number in range(1, Z // 2 + 1):
                line_copy(panel, way, hop_number).wait_send()
        for number in range(9):
            across(panel, number).wait_send()
    for s in range(LEAD_BLOCKS):
        away = lax.rem(z - s + Z, Z)
        for span in pieces_of(s, True) + pieces_of(s, False):
            for condition, copy in ring_sends(s, span, away):
                pl.when(condition)(copy.wait_send)
            for condition, copy in tree_sends(s, span):
                pl.when(condition & (away == 0))(copy.wait_send)


def whole(own, child, front, places, index_map):
    dma = pltpu.SemaphoreType.DMA
    f32, bf16 = jnp.float32, jnp.bfloat16
    return pl.pallas_call(
        front_kernel,
        out_shape=jax.ShapeDtypeStruct(front.shape, f32),
        in_specs=[VMEM, HBM, HBM, VMEM, VMEM],
        out_specs=VMEM,
        scratch_shapes=[
            pltpu.VMEM((LEAD_BLOCKS, BLOCK, LEAD), f32),
            pltpu.VMEM((LEAD_BLOCKS, BLOCK, LEAD + BLOCK), f32),
            pltpu.VMEM((BLOCK, BLOCK), f32),
            pltpu.VMEM((BLOCK, BLOCK), f32),
            pltpu.VMEM((LEAD_BLOCKS, BLOCK, BLOCK), f32),
            pltpu.VMEM(child.shape, f32),
            pltpu.VMEM((2, BLOCK, PANEL_WIDTH), bf16),
            pltpu.VMEM((Z * BLOCK, LEAD), bf16),
            pltpu.VMEM((STEPS * BLOCK, LEAD), bf16),
            pltpu.VMEM((STEPS, BLOCK, 4 * BLOCK), f32),
            pltpu.VMEM((STEPS, BLOCK, 4 * BLOCK), f32),
            pltpu.VMEM((2, BLOCK, 7 * BLOCK), f32),
            pltpu.VMEM((2, BLOCK, 7 * BLOCK), f32),
            pltpu.VMEM((2, BLOCK, 4 * BLOCK), f32),
            pltpu.VMEM((2, BLOCK, 4 * BLOCK), f32),
            pltpu.VMEM((BLOCK, child.shape[1]), f32),
            dma((2,)),
            dma((LEAD_BLOCKS, LEAD // PIECE, 2)),
            dma((LEAD // PIECE, 4)),
            dma((LEAD_BLOCKS, LEAD // PIECE)),
            dma((2,)),
            dma((2, 2)),
            dma((2, 2, Z // 2)),
            dma((2, 2, Z // 2)),
            dma((2, 9)),
            dma((2, 9)),
            dma((STEPS,)),
            dma((STEPS,)),
            dma((2,)),
            dma((2,)),
            dma((2,)),
            dma((2,)),
        ],
        compiler_params=pltpu.CompilerParams(
            collective_id=0, has_side_effects=True, vmem_limit_bytes=48 * MIB
        ),
        name="front",
    )(own, child, front, places, index_map)


def from_behind(shard, by):
    count = lax.axis_size("blk")
    return lax.ppermute(shard, "blk", [(i, (i + by) % count) for i in range(count)])


def contribution(tiles, places, own_places):
    slots = jnp.arange(BLOCK, dtype=jnp.int32)
    row_table = (places[..., None] == slots).astype(jnp.float32)
    shaped = tiles.reshape(TILE_WIDTH, -1, TILE_WIDTH)
    spread = jnp.einsum("cei,eiq->ceq", shaped, row_table, precision=HIGHEST)
    column_table = (own_places[..., None] == slots).astype(jnp.float32)
    return jnp.einsum(
        "cq,cn->qn", column_table, spread.reshape(TILE_WIDTH, -1), precision=HIGHEST
    )


def on_device(front, child, index_map):
    cycle = lax.axis_size("blk")
    half = cycle // 2
    index = lax.axis_index("blk")
    front, child = front[0], child[0]
    places = (index_map % BLOCK).reshape(cycle, TILE_WIDTH)
    own_places = lax.dynamic_index_in_dim(places, (index - half) % cycle, 0, keepdims=False)
    early = slice(half * TILE_WIDTH, (half + LEAD_BLOCKS) * TILE_WIDTH)
    early_tiles = from_behind(child[:, early], half)
    own = front[:, :LEAD] + contribution(
        early_tiles, places[half : half + LEAD_BLOCKS], own_places
    )
    return whole(own, child, front, own_places[None], index_map.reshape(-1, BLOCK))[None]


def solution(mesh):
    placed = (P("front", "blk", None), P("front", "blk", None), P("front"))
    return jax.shard_map(
        on_device, mesh=mesh, in_specs=placed, out_specs=P("front", "blk", None), check_vma=False
    )
```

```python
import jax
import jax.numpy as jnp
from jax import lax
from jax.experimental import pallas as pl
from jax.experimental.pallas import tpu as pltpu
from jax.sharding import PartitionSpec as P

PANEL_WIDTH = 512
BLOCK = 128
TILE_WIDTH = 64
LEAD = 2 * PANEL_WIDTH
LEAD_BLOCKS = LEAD // BLOCK
ROWS = 8
Z = 8
X = 4
PIECE = 128

HIGHEST = lax.Precision.HIGHEST
VMEM = pl.BlockSpec(memory_space=pltpu.VMEM)
HBM = pl.BlockSpec(memory_space=pltpu.HBM)
MIB = 1024 * 1024


def dot(a, b, dims=((1,), (0,)), precision=HIGHEST):
    return lax.dot_general(
        a, b, (dims, ((), ())), precision=precision, preferred_element_type=jnp.float32
    )


def position():
    me = lax.axis_index("blk")
    return me // (X * Z), me // Z % X, me % Z


def device(y, x, z):
    return {"blk": (y * X + lax.rem(x + X, X)) * Z + lax.rem(z + Z, Z)}


def remote(src, dst, send, recv, target):
    return pltpu.make_async_remote_copy(
        src_ref=src,
        dst_ref=dst,
        send_sem=send,
        recv_sem=recv,
        device_id=target,
        device_id_type=pl.DeviceIdType.MESH,
    )


def greet(partners):
    barrier = pltpu.get_barrier_semaphore()
    for partner in partners:
        pl.semaphore_signal(
            barrier, inc=1, device_id=partner, device_id_type=pl.DeviceIdType.MESH
        )
    pl.semaphore_wait(barrier, len(partners))


def spread_out(x):
    return jnp.broadcast_to(x, (ROWS, BLOCK))


def eliminate(parts, low, inv):
    done = []
    for r in range(ROWS):
        value = parts[r]
        for s in range(r):
            value = value - low[r][s] * done[s]
        done.append(value * inv[r])
    return done


def small_factor(cols):
    a = [[spread_out(cols[s][r : r + 1, :]) for s in range(r + 1)] for r in range(ROWS)]
    low = [[None] * ROWS for _ in range(ROWS)]
    inv = [None] * ROWS
    for s in range(ROWS):
        inv[s] = lax.rsqrt(a[s][s])
        for r in range(s + 1, ROWS):
            low[r][s] = a[r][s] * inv[s]
        for r in range(s + 1, ROWS):
            for t in range(s + 1, r + 1):
                a[r][t] = a[r][t] - low[r][s] * low[t][s]
    return low, inv


def invert_factor(a_ref, x_ref):
    row = lax.broadcasted_iota(jnp.int32, (BLOCK, BLOCK), 0)
    col = lax.broadcasted_iota(jnp.int32, (BLOCK, BLOCK), 1)
    x_ref[...] = jnp.where(row == col, 1.0, 0.0).astype(jnp.float32)
    for j in range(0, BLOCK, ROWS):
        w = a_ref[j : j + ROWS, :]
        e = x_ref[j : j + ROWS, :]
        low, inv = small_factor([spread_out(w[:, j + s : j + s + 1]) for s in range(ROWS)])
        y = eliminate([spread_out(w[r : r + 1, :]) for r in range(ROWS)], low, inv)
        f = eliminate([spread_out(e[r : r + 1, :]) for r in range(ROWS)], low, inv)
        for r in range(ROWS):
            x_ref[j + r : j + r + 1, :] = f[r][0:1, :]
        for i in range(j + ROWS, BLOCK, ROWS):
            block = a_ref[i : i + ROWS, :]
            other = x_ref[i : i + ROWS, :]
            z = eliminate(
                [spread_out(block[:, j + s : j + s + 1]) for s in range(ROWS)], low, inv
            )
            for s in range(ROWS):
                block = block - z[s] * y[s]
                other = other - z[s] * f[s]
            a_ref[i : i + ROWS, :] = block
            x_ref[i : i + ROWS, :] = other


PANEL_BLOCKS = PANEL_WIDTH // BLOCK
WIDTH = PANEL_WIDTH + BLOCK


def pieces_of(s, first):
    edges = [s * BLOCK] + [c for c in range(PIECE, LEAD + 1, PIECE) if c > s * BLOCK]
    spans = zip(edges[:-1], edges[1:])
    return [((c1 - 1) // PIECE, c0, c1) for c0, c1 in spans if (c1 <= PANEL_WIDTH) == first]


STEPS = 2 * X


def front_kernel(
    own_ref, child_ref, front_ref, places_ref, index_ref, out_ref,
    lead, work, a_ref, x_ref, inverses, tiles, staged,
    line, plane, made, came, z_made, z_came, two_made, two_came, picked,
    local_sem, b_send, a_send, b_recv, tile_sem, own_sem,
    l_send, l_recv, p_send, p_recv, q_send, q_recv, z_send, z_recv, two_send, two_recv,
):
    y, x, z = position()
    a = y * X + x
    over = device(1 - y, x, z)
    right, left = device(y, x + 1, z), device(y, x - 1, z)
    up, down = device(y, x, z + 1), device(y, x, z - 1)

    def plane_index(slot):
        return lax.rem(y + slot // X, 2) * X + lax.rem(x + lax.rem(slot, X), X)

    def plane_device(slot):
        return {"blk": plane_index(slot) * Z + z}

    up_two, down_two = device(y, x, z + 2), device(y, x, z - 2)
    greet([up, down, up_two, down_two] + [plane_device(slot) for slot in range(1, STEPS)])
    base = pltpu.make_async_copy(front_ref, out_ref, local_sem.at[1])
    base.start()
    root = a == 0

    def rows(slot, half=None):
        if half is None:
            return pl.ds(slot * BLOCK, BLOCK)
        return pl.ds(slot * BLOCK + half * (BLOCK // 2), BLOCK // 2)

    parts_of = ((0,), (1, 2))

    def part_columns(part):
        narrow = PANEL_WIDTH // 2
        return pl.ds(0, PANEL_WIDTH) if part == 0 else pl.ds((part + 1) * narrow, narrow)

    def own_copies(panel):
        return [
            pltpu.make_async_copy(
                staged.at[panel],
                target.at[rows(0), pl.ds(panel * PANEL_WIDTH, PANEL_WIDTH)],
                own_sem.at[panel, i],
            )
            for i, target in enumerate((line, plane))
        ]

    def keep_rows(panel):
        for i in range(PANEL_BLOCKS):
            s = panel * PANEL_BLOCKS + i
            q = lax.broadcasted_iota(jnp.int32, (BLOCK, BLOCK), 0) + s * BLOCK
            c = lax.broadcasted_iota(jnp.int32, (BLOCK, BLOCK), 1) + (a * Z + z) * BLOCK
            own = jnp.where(q <= c, work[s, :, PANEL_WIDTH:WIDTH], 0.0)
            staged[panel, :, i * BLOCK : (i + 1) * BLOCK] = own.T.astype(jnp.bfloat16)
        for copy in own_copies(panel):
            copy.start()

    def line_copy(part, way, hop):
        half = None if hop < Z // 2 else way
        sign = -1 if way == 0 else 1
        start, end = (sign * (hop - 1)) % Z, (sign * hop) % Z
        return remote(
            line.at[rows(start, half), part_columns(part)],
            line.at[rows(end, half), part_columns(part)],
            l_send.at[part, way, hop - 1],
            l_recv.at[part, way, hop - 1],
            up if way == 0 else down,
        )

    def across(part, number):
        start, end, half, target = [
            (0, 4, None, over),
            (0, 3, None, right),
            (0, 1, None, left),
            (4, 7, None, right),
            (4, 5, None, left),
            (3, 2, 0, right),
            (1, 2, 1, left),
            (7, 6, 0, right),
            (5, 6, 1, left),
        ][number]
        return remote(
            plane.at[rows(start, half), part_columns(part)],
            plane.at[rows(end, half), part_columns(part)],
            p_send.at[part, number],
            p_recv.at[part, number],
            target,
        )

    def gather(panel):
        along, beside = own_copies(panel)
        along.wait()
        for part in parts_of[panel]:
            line_copy(part, 0, 1).start()
            line_copy(part, 1, 1).start()
        beside.wait()
        for part in parts_of[panel]:
            for number in (0, 1, 2):
                across(part, number).start()

    def pass_on(part, hop):
        for way in (0, 1):
            line_copy(part, way, hop).wait_recv()
            line_copy(part, way, hop + 1).start()

    def pass_across(part, number, *onward):
        across(part, number).wait_recv()
        for other in onward:
            across(part, other).start()

    def gather_first(part):
        pass_on(part, 1)
        pass_across(part, 0, 3, 4)
        pass_across(part, 1, 5)
        pass_across(part, 2, 6)

    def gather_second(part):
        pass_on(part, 2)
        pass_across(part, 3, 7)
        pass_across(part, 4, 8)

    def gather_third(part):
        pass_on(part, 3)

    def gather_last(part):
        for number in (5, 6, 7, 8):
            across(part, number).wait_recv()
        for way in (0, 1):
            line_copy(part, way, Z // 2).wait_recv()

    def piece(s, span, send, target):
        p, c0, c1 = span
        part = lead.at[s, :, c0:c1]
        return remote(part, part, send, b_recv.at[s, p], target)

    def tree_sends(s, span):
        p = span[0]
        onward = (x == 1) if p % 2 == 0 else (x == 3)
        return [
            (root, piece(s, span, a_send.at[p, 0], over)),
            (x == 0, piece(s, span, a_send.at[p, 1], right)),
            (x == 0, piece(s, span, a_send.at[p, 2], left)),
            (onward, piece(s, span, a_send.at[p, 3], right if p % 2 == 0 else left)),
        ]

    def ring_sends(s, span, away):
        p = span[0]
        ups = Z // 2 if s % 2 == 0 else Z // 2 - 1
        go_up = away < ups
        go_down = (away == 0) | (away > ups + 1)
        return [
            (go_up, piece(s, span, b_send.at[s, p, 0], up)),
            (go_down, piece(s, span, b_send.at[s, p, 1], down)),
        ]

    def start(sends):
        for condition, copy in sends:
            pl.when(condition)(copy.start)

    def arrived(s, span):
        piece(s, span, b_send.at[s, span[0], 0], up).wait_recv()

    def each_slab(slab, first, act):
        for s in range(LEAD_BLOCKS):
            spans = pieces_of(s, first)
            if spans:

                @pl.when(slab == s)
                def _(s=s, spans=spans):
                    for span in spans:
                        act(s, span)

    def tree(first):
        def act(s, span):
            pl.when(jnp.logical_not(root))(lambda: arrived(s, span))
            start(tree_sends(s, span))
            if first:
                start(ring_sends(s, span, 0))

        each_slab(z, first, act)

    def hop(t, first):
        away = jnp.where(lax.rem(t, 2) == 1, (t + 1) // 2, Z - t // 2)

        def act(s, span):
            arrived(s, span)
            start(ring_sends(s, span, away))

        each_slab(lax.rem(z - away + Z, Z), first, act)

    @pl.when(root)
    def _():
        copy = pltpu.make_async_copy(own_ref, lead.at[z], local_sem.at[0])
        copy.start()
        copy.wait()

    tree(True)
    level = y + jnp.where(x == 0, 0, 1) + jnp.where(x == 2, 1, 0)
    turn = jnp.where(level == 0, 1, jnp.where(level == 1, 3, jnp.where(level == 2, 6, 8)))
    for s in range(LEAD_BLOCKS):
        own_part = own_ref[:, s * BLOCK : (s + 1) * BLOCK].T
        work[s, :, PANEL_WIDTH:WIDTH] = own_part

    def first_hops(t, carry):
        pl.when(t == turn)(lambda: tree(False))
        pl.when(t < Z)(lambda: hop(t, True))
        return carry

    lax.fori_loop(1, Z + 1, first_hops, 0)
    each_slab(z, False, lambda s, span: start(ring_sends(s, span, 0)))
    for s in range(PANEL_BLOCKS):
        work[s, :, 0:PANEL_WIDTH] = lead[s, :, 0:PANEL_WIDTH]

    tiles_copy = remote(child_ref, tiles, tile_sem.at[0], tile_sem.at[1], over)

    def step(b, carry):
        panel = b // PANEL_BLOCKS
        window = pl.ds(pl.multiple_of(panel * PANEL_WIDTH, BLOCK), WIDTH)

        def block(t):
            return pl.ds(pl.multiple_of((t + panel) * BLOCK, BLOCK), BLOCK)

        @pl.when((b > 0) & (b < PANEL_BLOCKS))
        def _():
            def act(t, carry):
                hop(t, False)
                return carry

            lax.fori_loop(2 * b - 1, 2 * b + 1, act, 0)

        pl.when(b == 2)(tiles_copy.start)
        pl.when(b == PANEL_BLOCKS + 1)(lambda: gather_first(0))
        pl.when(b == PANEL_BLOCKS + 2)(lambda: gather_third(0))
        a_ref[...] = work[b, :, block(b)]
        invert_factor(a_ref, x_ref)
        inverses[b] = x_ref[...]
        pl.when(b == PANEL_BLOCKS)(lambda: gather(0))
        pl.when(b == PANEL_BLOCKS + 1)(lambda: gather_second(0))
        work[b, :, window] = dot(x_ref[...], work[b, :, window])

        def update(t, carry):
            crossing = work[b, :, block(t)]
            work[t, :, window] = work[t, :, window] - dot(crossing, work[b, :, window], ((0,), (0,)))
            return carry

        lax.fori_loop(b + 1, (panel + 1) * PANEL_BLOCKS, update, 0)

        @pl.when(b == PANEL_BLOCKS - 1)
        def _():
            hop(jnp.full((), Z - 1, jnp.int32), False)
            for s in range(LEAD_BLOCKS):
                work[s, :, WIDTH:] = lead[s, :, PANEL_WIDTH:LEAD]

            def solve(s, carry):
                work[s, :, WIDTH:] = dot(inverses[s], work[s, :, WIDTH:])

                def update(t, carry):
                    crossing = work[s, :, pl.ds(pl.multiple_of(t * BLOCK, BLOCK), BLOCK)]
                    rest = dot(crossing, work[s, :, WIDTH:], ((0,), (0,)))
                    work[t, :, WIDTH:] = work[t, :, WIDTH:] - rest
                    return carry

                lax.fori_loop(s + 1, PANEL_BLOCKS, update, 0)
                return carry

            lax.fori_loop(0, PANEL_BLOCKS, solve, 0)
            first = work[0:PANEL_BLOCKS, :, PANEL_WIDTH:].astype(jnp.bfloat16)
            first = first.reshape(PANEL_WIDTH, WIDTH)
            for t in range(PANEL_BLOCKS):
                rows = work[PANEL_BLOCKS + t, :, PANEL_WIDTH:]
                crossing = first[:, (t + 1) * BLOCK : (t + 2) * BLOCK]
                work[PANEL_BLOCKS + t, :, PANEL_WIDTH:] = rows - dot(
                    crossing, first, ((0,), (0,)), None
                )
            keep_rows(0)

        return carry

    lax.fori_loop(0, LEAD_BLOCKS, step, 0)
    keep_rows(1)
    gather(1)
    for act in (gather_first, gather_second, gather_third):
        for part in parts_of[1]:
            act(part)
    for part in (0, 1, 2):
        gather_last(part)

    def lefts(block, holder, zz):
        j = lax.broadcasted_iota(jnp.int32, (BLOCK, LEAD), 0) + lax.rem(zz + Z, Z) * BLOCK
        q = lax.broadcasted_iota(jnp.int32, (BLOCK, LEAD), 1)
        chosen = jnp.where(j == q, 1.0, 0.0).astype(jnp.bfloat16)
        is_lead = jnp.full((BLOCK, LEAD), holder, jnp.int32) == 0
        return jnp.where(is_lead, chosen, block)

    def product(left_side, right_side):
        return dot(left_side, right_side, ((1,), (1,)), None)

    def first_of(slot):
        return jnp.where(slot < X, 2, 3)

    def product_copy(slot):
        landing = slot // X * X + lax.rem(X - lax.rem(slot, X), X)
        return remote(
            made.at[slot], came.at[landing], q_send.at[slot], q_recv.at[landing], plane_device(slot)
        )

    def z_copy(way):
        return remote(
            z_made.at[way],
            z_came.at[way],
            z_send.at[way],
            z_recv.at[way],
            up if way == 0 else down,
        )

    two_slots = (range(1, X), range(X, STEPS))

    def two_copy(way):
        width = len(two_slots[way]) * BLOCK
        return remote(
            two_made.at[way, :, 0:width],
            two_came.at[way, :, 0:width],
            two_send.at[way],
            two_recv.at[way],
            up_two if way == 0 else down_two,
        )

    sends = a != 0

    def slot_at(i):
        return lax.rem(i * 5, STEPS)

    def make(i, carry):
        slot = slot_at(i)
        block = plane[pl.ds(pl.multiple_of(slot * BLOCK, BLOCK), BLOCK)]
        part = line[pl.ds(pl.multiple_of(first_of(slot) * BLOCK, BLOCK), 4 * BLOCK)]
        made[slot] = product(lefts(block, plane_index(slot), z), part)

        @pl.when(sends & (i > 1))
        def _():
            product_copy(slot_at(i - 1)).start()

        return carry

    lax.fori_loop(1, STEPS, make, 0)
    two_made[0, :, 0 : (X - 1) * BLOCK] = product(
        lefts(line[rows(2)], a, z + 2), plane[BLOCK : X * BLOCK]
    )
    pl.when(sends)(product_copy(slot_at(jnp.full((), STEPS - 1, jnp.int32))).start)
    two_made[1] = product(lefts(line[rows(Z - 2)], a, z - 2), plane[X * BLOCK :])
    two_copy(0).start()
    z_made[0] = product(lefts(line[rows(1)], a, z + 1), plane[BLOCK:])
    two_copy(1).start()
    z_made[1] = product(lefts(line[rows(Z - 1)], a, z - 1), plane[BLOCK:])
    z_copy(0).start()

    def put(aa, zz, value):
        block = aa * Z + lax.rem(zz + Z, Z)
        columns = pl.ds(pl.multiple_of(block * BLOCK, BLOCK), BLOCK)
        kept = jnp.where(jnp.full((BLOCK, BLOCK), aa, jnp.int32) == 0, 0.0, out_ref[:, columns] - value)
        is_lead = jnp.full((BLOCK, BLOCK), a, jnp.int32) == 0
        out_ref[:, columns] = jnp.where(is_lead, value, kept)

    own = lefts(line[rows(0)], a, z)
    along = product(own, line[...])
    z_copy(1).start()
    base.wait()
    tiles_copy.wait_recv()
    slot_of = lax.broadcasted_iota(jnp.int32, (BLOCK, TILE_WIDTH), 0)
    column_table = jnp.where(slot_of == places_ref[...], 1.0, 0.0).astype(jnp.float32)
    order = picked.shape[1]
    for start in range(0, order, LEAD):
        picked[:, start : start + LEAD] = dot(column_table, tiles[:, start : start + LEAD])
    pairs = order // BLOCK

    def place(pair, carry):
        start = lax.rem(pair + pairs // 2, pairs) * (2 * BLOCK)
        slot = lax.broadcasted_iota(jnp.int32, (2 * BLOCK, BLOCK), 0) + start
        row_table = jnp.where(slot == index_ref[pl.ds(pair, 1), :], 1.0, 0.0).astype(jnp.float32)
        part = picked[:, pl.ds(pl.multiple_of(pair * BLOCK, BLOCK), BLOCK)]
        columns = pl.ds(pl.multiple_of(start, BLOCK), 2 * BLOCK)
        out_ref[:, columns] = out_ref[:, columns] + dot(part, row_table, ((1,), (1,)))
        return carry

    lax.fori_loop(0, pairs, place, 0)
    for s in range(Z):
        put(a, z + s, along[:, s * BLOCK : (s + 1) * BLOCK])
    along = product(own, plane[BLOCK:])
    for slot in range(1, STEPS):
        put(plane_index(slot), z, along[:, (slot - 1) * BLOCK : slot * BLOCK])
    for way in (0, 1):
        z_copy(way).wait_recv()
        for slot in range(1, STEPS):
            value = z_came[way, :, (slot - 1) * BLOCK : slot * BLOCK]
            put(plane_index(slot), z - 1 if way == 0 else z + 1, value)
    for way in (0, 1):
        two_copy(way).wait_recv()
        for i, slot in enumerate(two_slots[way]):
            value = two_came[way, :, i * BLOCK : (i + 1) * BLOCK]
            put(plane_index(slot), z - 2 if way == 0 else z + 2, value)

    def take(i, carry):
        slot = slot_at(i)
        source = plane_index(slot)

        @pl.when(source != 0)
        def _():
            landing = slot // X * X + lax.rem(X - lax.rem(slot, X), X)
            product_copy(landing).wait_recv()
            for s in range(4):
                value = came[slot, :, s * BLOCK : (s + 1) * BLOCK]
                put(source, z + first_of(slot) + s, value)

        @pl.when(source == 0)
        def _():
            for s in range(4):
                zz = lax.rem(z + first_of(slot) + s, Z)
                columns = pl.ds(pl.multiple_of(zz * BLOCK, BLOCK), BLOCK)
                out_ref[:, columns] = jnp.zeros((BLOCK, BLOCK), jnp.float32)

        return carry

    lax.fori_loop(1, STEPS, take, 0)
    for slot in range(1, STEPS):
        pl.when(sends)(product_copy(slot).wait_send)
    for way in (0, 1):
        z_copy(way).wait_send()
        two_copy(way).wait_send()
    tiles_copy.wait_send()
    for part in (0, 1, 2):
        for way in (0, 1):
            for hop_number in range(1, Z // 2 + 1):
                line_copy(part, way, hop_number).wait_send()
        for number in range(9):
            across(part, number).wait_send()
    for s in range(LEAD_BLOCKS):
        away = lax.rem(z - s + Z, Z)
        for span in pieces_of(s, True) + pieces_of(s, False):
            for condition, copy in ring_sends(s, span, away):
                pl.when(condition)(copy.wait_send)
            for condition, copy in tree_sends(s, span):
                pl.when(condition & (away == 0))(copy.wait_send)


def whole(own, child, front, places, index_map):
    dma = pltpu.SemaphoreType.DMA
    f32, bf16 = jnp.float32, jnp.bfloat16
    return pl.pallas_call(
        front_kernel,
        out_shape=jax.ShapeDtypeStruct(front.shape, f32),
        in_specs=[VMEM, HBM, HBM, VMEM, VMEM],
        out_specs=VMEM,
        scratch_shapes=[
            pltpu.VMEM((LEAD_BLOCKS, BLOCK, LEAD), f32),
            pltpu.VMEM((LEAD_BLOCKS, BLOCK, LEAD + BLOCK), f32),
            pltpu.VMEM((BLOCK, BLOCK), f32),
            pltpu.VMEM((BLOCK, BLOCK), f32),
            pltpu.VMEM((LEAD_BLOCKS, BLOCK, BLOCK), f32),
            pltpu.VMEM(child.shape, f32),
            pltpu.VMEM((2, BLOCK, PANEL_WIDTH), bf16),
            pltpu.VMEM((Z * BLOCK, LEAD), bf16),
            pltpu.VMEM((STEPS * BLOCK, LEAD), bf16),
            pltpu.VMEM((STEPS, BLOCK, 4 * BLOCK), f32),
            pltpu.VMEM((STEPS, BLOCK, 4 * BLOCK), f32),
            pltpu.VMEM((2, BLOCK, 7 * BLOCK), f32),
            pltpu.VMEM((2, BLOCK, 7 * BLOCK), f32),
            pltpu.VMEM((2, BLOCK, 4 * BLOCK), f32),
            pltpu.VMEM((2, BLOCK, 4 * BLOCK), f32),
            pltpu.VMEM((BLOCK, child.shape[1]), f32),
            dma((2,)),
            dma((LEAD_BLOCKS, LEAD // PIECE, 2)),
            dma((LEAD // PIECE, 4)),
            dma((LEAD_BLOCKS, LEAD // PIECE)),
            dma((2,)),
            dma((2, 2)),
            dma((3, 2, Z // 2)),
            dma((3, 2, Z // 2)),
            dma((3, 9)),
            dma((3, 9)),
            dma((STEPS,)),
            dma((STEPS,)),
            dma((2,)),
            dma((2,)),
            dma((2,)),
            dma((2,)),
        ],
        compiler_params=pltpu.CompilerParams(
            collective_id=0, has_side_effects=True, vmem_limit_bytes=48 * MIB
        ),
        name="front",
    )(own, child, front, places, index_map)


def from_behind(shard, by):
    count = lax.axis_size("blk")
    return lax.ppermute(shard, "blk", [(i, (i + by) % count) for i in range(count)])


def contribution(tiles, places, own_places):
    slots = jnp.arange(BLOCK, dtype=jnp.int32)
    row_table = (places[..., None] == slots).astype(jnp.float32)
    shaped = tiles.reshape(TILE_WIDTH, -1, TILE_WIDTH)
    spread = jnp.einsum("cei,eiq->ceq", shaped, row_table, precision=HIGHEST)
    column_table = (own_places[..., None] == slots).astype(jnp.float32)
    return jnp.einsum(
        "cq,cn->qn", column_table, spread.reshape(TILE_WIDTH, -1), precision=HIGHEST
    )


def on_device(front, child, index_map):
    cycle = lax.axis_size("blk")
    half = cycle // 2
    index = lax.axis_index("blk")
    front, child = front[0], child[0]
    places = (index_map % BLOCK).reshape(cycle, TILE_WIDTH)
    own_places = lax.dynamic_index_in_dim(places, (index - half) % cycle, 0, keepdims=False)
    early = slice(half * TILE_WIDTH, (half + LEAD_BLOCKS) * TILE_WIDTH)
    early_tiles = from_behind(child[:, early], half)
    own = front[:, :LEAD] + contribution(
        early_tiles, places[half : half + LEAD_BLOCKS], own_places
    )
    return whole(own, child, front, own_places[None], index_map.reshape(-1, BLOCK))[None]


def solution(mesh):
    placed = (P("front", "blk", None), P("front", "blk", None), P("front"))
    return jax.shard_map(
        on_device, mesh=mesh, in_specs=placed, out_specs=P("front", "blk", None), check_vma=False
    )
```
